32 devices in a mesh: win: 2 (over x), sub: 16 (over z, y, core).
Axes of the slice: x: 2, y: 2, z: 4, core: 2. Of those that a mesh axis runs over, the one named last changes fastest.
Arguments:
- pulses: bfloat16 [32, 80, 2, 4096], P(('win', 'sub')), parts along dimension 0, may hold values from -6 to 6
- offsets: int32 [32, 80], P(('win', 'sub')), parts along dimension 0, may hold values from 0 to 3968
- geometry: float32 [32, 3, 80], P(('win', 'sub')), parts along dimension 0, may hold values from -1 to 1
- counts: int32 [32], P(('win', 'sub')), parts along dimension 0, may hold values from 48 to 80, as said below
Outputs:
- frames: float32 [32, 2, 32, 512], P(('win', 'sub')), parts along dimension 0
- cumulative: float32 [32, 2, 32, 512], P(('win', 'sub')), parts along dimension 0
The draws below stay inside these ranges and needn't reach their ends.
There are 2 independent parts, one for each index of `win`. The reference program is written for one: setup_inputs(seed, part) draws one part's arguments, and reference() takes and returns one part's arrays. A program takes and returns all parts, laid end to end along the dimension named above; each array names one. Nothing has to cross between parts.
Inputs may be any that keep to these rules, and one draw needn't show every extreme that they name: Subaperture s holds its pulses in slots 0 to counts[s] - 1; the other slots are unused. Some subaperture has 80 pulses and some 48.
All inputs are finite; a program needn't handle non-finite values.
Results may differ from the reference program's by a relative error of at most 0.004.
Values sent between devices are 32-bit elements; how exact they have to be, the bound alone decides.
A program may use at most 192 MiB of HBM per device.

```python
import math
import jax
import jax.numpy as jnp
from jax import lax

ROWS = 32
COLS = 512
SAMPLES = 4096
BINS = 128
PULSES = 80
FEWEST = 48
SUBAPS = 16


def draw_counts(key, part):
    first_key, second_key = jax.random.split(jax.random.fold_in(key, 7071))
    base = jax.random.randint(first_key, (SUBAPS,), FEWEST, PULSES + 1, dtype=jnp.int32)
    order = jax.random.permutation(second_key, SUBAPS)
    base = base.at[order[0]].set(PULSES)
    base = base.at[order[1]].set(FEWEST)
    return base.astype(jnp.int32)


def touch_ends(entries, stream_key, low, top_value):
    index_at = [jax.random.randint(jax.random.fold_in(stream_key, axis), (), 0, length) for axis, length in enumerate(entries.shape)]
    main_axis = entries.shape.index(max(entries.shape))
    neighbour = index_at[:main_axis] + [(index_at[main_axis] + 1) % entries.shape[main_axis]] + index_at[main_axis + 1:]
    return entries.at[tuple(index_at)].set(low).at[tuple(neighbour)].set(top_value)


def shard_levels(stream_key, shape, pieces, smallest, high):
    level = 1.0
    for axis_at, blocks in pieces:
        heights = jax.random.uniform(jax.random.fold_in(jax.random.fold_in(stream_key, 6), axis_at), (blocks,), jnp.float32, smallest / len(pieces), high / len(pieces))
        level = level * jnp.repeat(jnp.exp(heights), shape[axis_at] // blocks).reshape((-1,) + (1,) * (len(shape) - 1 - axis_at))
    return level


def noise(key, extent, deviation, reach, pieces=(), held_as=jnp.bfloat16):
    drawn = deviation * jax.random.normal(key, extent, jnp.float32)
    if pieces:
        drawn = drawn * shard_levels(key, extent, pieces, -0.22, 0.18)
    return jnp.clip(drawn, -reach, reach).astype(held_as)


def setup_inputs(seed: int = 0, part: int = 0) -> dict:
    splits = jax.random.split(jax.random.key(seed), 5)
    own_keys = jax.random.split(jax.random.fold_in(splits[4], part), 5)
    return {
        "pulses": noise(own_keys[0], (SUBAPS, PULSES, 2, SAMPLES), 1.0, 6.0, ((0, 16),)),
        "offsets": touch_ends(jax.random.randint(own_keys[1], (SUBAPS, PULSES), 0, SAMPLES - BINS + 1), jax.random.fold_in(own_keys[1], 1), 0, SAMPLES - BINS).astype(jnp.int32),
        "geometry": jnp.clip(jax.random.uniform(own_keys[2], (SUBAPS, 3, PULSES), jnp.float32, -1.0, 1.0) * shard_levels(own_keys[2], (SUBAPS, 3, PULSES), ((0, 16),), -0.4, 0.0), -1.0, 1.0),
        "counts": draw_counts(jax.random.fold_in(jax.random.fold_in(splits[4], part), 71), part),
    }


def spectrum_of(pulse_rows, vertical_offset_along, geometry_sub, count, width):
    slots = pulse_rows.shape[0]
    windows = jax.vmap(lambda one_row, offset: lax.dynamic_slice_in_dim(one_row, offset, width, 1))(pulse_rows, vertical_offset_along.astype(jnp.int32)).astype(jnp.float32)
    index = jnp.arange(width, dtype=jnp.int32)
    shifted = index - width // 2
    turns = index[:, None] * shifted[None, :] % width
    angle = 2.0 * math.pi / width * turns.astype(jnp.float32)
    cosine = jnp.cos(angle)
    sine = jnp.sin(angle)
    highest = lax.Precision.HIGHEST
    real_in = windows[:, 0]
    imag_in = windows[:, 1]
    real_out = (jnp.dot(real_in, cosine, precision=highest) + jnp.dot(imag_in, sine, precision=highest)) / width
    imag_out = (jnp.dot(imag_in, cosine, precision=highest) - jnp.dot(real_in, sine, precision=highest)) / width
    viewing_bearing = 2.0 * math.pi * (shifted.astype(jnp.float32) / width + 0.37)
    scene_middle = width / 2.0 + width / 16.0 * geometry_sub[0]
    radar_frequency = 2.0 * math.pi / 100.0 * (37 * vertical_offset_along % 100).astype(jnp.float32)
    signal_argument = viewing_bearing[None, :] * scene_middle[:, None] + radar_frequency[:, None]
    live = (jnp.arange(slots, dtype=jnp.int32) < count).astype(jnp.float32) / math.sqrt(slots)
    cos_phase = jnp.cos(signal_argument)
    sin_phase = jnp.sin(signal_argument)
    coefficient_real = live[:, None] * (real_out * cos_phase - imag_out * sin_phase)
    coef_im = live[:, None] * (real_out * sin_phase + imag_out * cos_phase)
    return (coefficient_real, coef_im, viewing_bearing)

def block_product(coefficient_real, coef_im, viewing_bearing, row_slope, column_gradient, rows, cols):
    xpos = (jnp.arange(rows, dtype=jnp.int32) - rows // 2).astype(jnp.float32)
    ypos = (jnp.arange(cols, dtype=jnp.int32) - cols // 2).astype(jnp.float32)
    angle_x = xpos[:, None, None] * (viewing_bearing[None, :] * row_slope[:, None])[None]
    cosine_x = jnp.cos(angle_x)
    sine_x = jnp.sin(angle_x)
    left_re = coefficient_real[None] * cosine_x - coef_im[None] * sine_x
    left_im = coefficient_real[None] * sine_x + coef_im[None] * cosine_x
    left = jnp.concatenate([left_re.reshape(rows, -1), left_im.reshape(rows, -1)], axis=1).astype(jnp.bfloat16)
    angle_y = (viewing_bearing[None, :] * column_gradient[:, None])[:, :, None] * ypos[None, None, :]
    right_re = jnp.cos(angle_y).reshape(-1, cols)
    right_im = jnp.sin(angle_y).reshape(-1, cols)
    upper = jnp.concatenate([right_re, right_im], axis=1)
    lower = jnp.concatenate([-right_im, right_re], axis=1)
    right = jnp.concatenate([upper, lower], axis=0).astype(jnp.bfloat16)
    return jnp.dot(left, right, preferred_element_type=jnp.float32)

def single_picture(pulse_rows, vertical_offset_along, geometry_sub, count):
    coefficient_real, coef_im, viewing_bearing = spectrum_of(pulse_rows, vertical_offset_along, geometry_sub, count, BINS)
    row_slope = 0.05 * geometry_sub[1]
    column_gradient = 0.05 * geometry_sub[2]

    def add_block(step, total):
        start = (step * 8).astype(jnp.int32)
        part_re = lax.dynamic_slice_in_dim(coefficient_real, start, 8, 0)
        part_im = lax.dynamic_slice_in_dim(coef_im, start, 8, 0)
        slope_r = lax.dynamic_slice_in_dim(row_slope, start, 8, 0)
        slope_c = lax.dynamic_slice_in_dim(column_gradient, start, 8, 0)
        return total + block_product(part_re, part_im, viewing_bearing, slope_r, slope_c, ROWS, COLS)
    total = lax.fori_loop(0, PULSES // 8, add_block, jnp.zeros((ROWS, 2 * COLS), jnp.float32))
    return jnp.stack([total[:, :COLS], total[:, COLS:]], axis=0)

def reference(pulses, offsets, geometry, counts):
    image_frames = lax.map(lambda items: single_picture(items[0], items[1], items[2], items[3]), (pulses, offsets, geometry, counts))
    prefix = jnp.cumsum(image_frames, axis=0)
    lagged = jnp.concatenate([jnp.zeros((8,) + prefix.shape[1:], jnp.float32), prefix[:-8]], axis=0)
    frames = (prefix - lagged) / math.sqrt(8.0)
    scale = jnp.sqrt(jnp.arange(1, SUBAPS + 1, dtype=jnp.int32).astype(jnp.float32))
    cumulative = prefix / scale[:, None, None, None]
    return (frames, cumulative)
```

```python
import functools
import math

import jax
import jax.numpy as jnp
import numpy as np
from jax import lax
from jax.experimental import pallas as pl
from jax.experimental.pallas import tpu as pltpu
from jax.sharding import PartitionSpec as P

ROWS = 32
COLS = 512
BINS = 128
GROUP = 4
HIGHEST = lax.Precision.HIGHEST

_N = 4001


def _sine_series():
    u = 0.25 * np.cos(np.pi * (np.arange(_N) + 0.5) / _N)
    basis = np.stack([u ** (2 * k + 1) for k in range(6)], axis=1)
    scale = np.abs(basis).max(axis=0)
    fit = np.linalg.lstsq(basis / scale, np.sin(2.0 * np.pi * u), rcond=None)[0] / scale
    return [float(np.float32(c)) for c in fit]


SINE = _sine_series()


def quarter_sine(u):
    z = u * u
    total = SINE[5]
    for k in (4, 3, 2, 1, 0):
        total = total * z + SINE[k]
    return total * u


def cos_sin(turns):
    r = turns - jnp.round(turns)
    a = jnp.abs(r)
    s = quarter_sine(jnp.minimum(a, 0.5 - a))
    return quarter_sine(0.25 - a), jnp.where(r < 0, -s, s)


def frequency_order(width):
    order = []
    for j in range(width // 16):
        order += [16 * j + 8 + l for l in range(8)] + [16 * j + 7 - l for l in range(8)]
    return np.array(order)


def tables(width, rows, cols):
    order = frequency_order(width)
    g = order - width // 2
    b = np.arange(width)
    angle = 2.0 * np.pi * ((b[:, None] * g[None, :]) % width) / width
    dft = np.concatenate([np.cos(angle), np.sin(angle)], axis=1) / width
    tau = g / width + 0.37
    m = np.arange(1, cols // 2 + 1)
    l = np.arange(8)
    middles = (16 * np.arange(width // 16) + 7.5 - width // 2) / width + 0.37
    side = ((l + 0.5) / width)[:, None] * m[None, :] * 0.05
    middle = middles[:, None] * m[None, :] * 0.05
    row = l[:, None] * tau[None, :] * 0.05
    lead = np.stack([tau, g], axis=0)
    f32 = np.float32
    return (
        dft.astype(f32),
        np.concatenate([side, middle], axis=0).astype(f32),
        row.astype(f32),
        lead.astype(f32),
    )


def own_image(
    offs_s, geo_s, count_s, pulses, offs_v, geo_v, dft, column, row, lead, win, coef, acc, rows, cols
):
    slots, width = pulses.shape[1], dft.shape[0]
    half = cols // 2
    last = pulses.shape[3] // width - 2
    lanes = lax.broadcasted_iota(jnp.int32, (2, width), 1)

    def fetch(p):
        offset = offs_s[0, p]
        block = jnp.minimum(offset // width, last)
        rest = offset - block * width
        first = pulses[0, p, :, pl.ds(pl.multiple_of(block * width, width), width)]
        second = pulses[0, p, :, pl.ds(pl.multiple_of(block * width + width, width), width)]
        both = jnp.where(
            lanes >= rest, first.astype(jnp.float32), second.astype(jnp.float32)
        )
        win[pl.ds(p, 1), :] = both[0:1]
        win[pl.ds(slots + p, 1), :] = both[1:2]

    def fetch_some(i, _):
        for k in range(8):
            fetch(i * 8 + k)
        return 0

    lax.fori_loop(0, slots // 8, fetch_some, 0)

    out = jnp.dot(win[...], dft[...], precision=HIGHEST, preferred_element_type=jnp.float32)
    spec_re = out[:slots, :width] + out[slots:, width:]
    spec_im = out[slots:, :width] - out[:slots, width:]

    eye = lax.broadcasted_iota(jnp.int32, (slots, slots), 0) == lax.broadcasted_iota(
        jnp.int32, (slots, slots), 1
    )

    def upright(line):
        return jnp.sum(jnp.where(eye, line, 0.0), axis=1, keepdims=True)

    offset_line = offs_v[...]
    block_line = jnp.minimum(offset_line // width, last)
    rest = upright((offset_line - block_line * width).astype(jnp.float32))
    carrier = upright((37 * offset_line % 100).astype(jnp.float32) / 100.0)
    centre = width / 2.0 + width / 16.0 * upright(geo_v[0, 0:1, :])
    slope = 0.05 * upright(geo_v[0, 1:2, :])
    tau = lead[0:1, :]
    turned = lead[1:2, :] * rest * (1.0 / width)
    phase = tau * centre
    phase = (phase - jnp.round(phase)) + carrier + (turned - jnp.round(turned))
    live = jnp.where(
        lax.broadcasted_iota(jnp.int32, (slots, 1), 0) < count_s[0], 1.0 / math.sqrt(slots), 0.0
    )
    spec_re = spec_re * live
    spec_im = spec_im * live
    blocks = rows // 8
    for q in range(blocks):
        c, s = cos_sin(phase + tau * slope * float(8 * q - rows // 2))
        coef[2 * q] = spec_re * c - spec_im * s
        coef[2 * q + 1] = spec_re * s + spec_im * c

    acc[...] = jnp.zeros_like(acc)

    def pulse(p):
        cx, sx = cos_sin(row[...] * geo_s[0, 1, p])
        real, imag = [], []
        for q in range(blocks):
            cr = coef[2 * q, pl.ds(p, 1), :]
            ci = coef[2 * q + 1, pl.ds(p, 1), :]
            real.append(cr * cx - ci * sx)
            imag.append(cr * sx + ci * cx)
        left = jnp.concatenate(real + imag, axis=0).astype(jnp.bfloat16)
        cy, sy = cos_sin(column[...] * geo_s[0, 2, p])
        c0, s0 = cy[:8], sy[:8]
        right_c, right_s = [], []
        for j in range(width // 16):
            cm, sm = cy[8 + j : 9 + j], sy[8 + j : 9 + j]
            cc, ss, sc, cs = cm * c0, sm * s0, sm * c0, cm * s0
            right_c += [cc - ss, cc + ss]
            right_s += [sc + cs, sc - cs]
        right = jnp.concatenate(
            [
                jnp.concatenate(right_c, axis=0).astype(jnp.bfloat16),
                jnp.concatenate(right_s, axis=0).astype(jnp.bfloat16),
            ],
            axis=1,
        )
        return left, right

    def step(i, total):
        lefts, rights = [], []
        for k in range(GROUP):
            left, right = pulse(i * GROUP + k)
            total = total + left.astype(jnp.float32)
            lefts.append(left)
            rights.append(right)
        acc[...] += jnp.dot(
            jnp.concatenate(lefts, axis=1),
            jnp.concatenate(rights, axis=0),
            preferred_element_type=jnp.float32,
        )
        return total

    total = lax.fori_loop(
        0, slots // GROUP, step, jnp.zeros((2 * rows, width), jnp.float32)
    )
    zero = jnp.sum(total, axis=1, keepdims=True)
    rc, rs = acc[:rows, :half], acc[:rows, half:]
    ic, is_ = acc[rows:, :half], acc[rows:, half:]
    ahead = jnp.concatenate([rc - is_, rs + ic], axis=0)
    behind = jnp.concatenate([rc + is_, ic - rs], axis=0)
    flip = (
        lax.broadcasted_iota(jnp.int32, (half, half), 0)
        + lax.broadcasted_iota(jnp.int32, (half, half), 1)
        == half - 1
    ).astype(jnp.float32)
    low = jnp.dot(behind, flip, precision=HIGHEST, preferred_element_type=jnp.float32)
    high = pltpu.roll(ahead, 1, 1)
    high = jnp.where(lax.broadcasted_iota(jnp.int32, high.shape, 1) == 0, zero, high)
    return low, high


def image_kernel(
    offs_s, geo_s, count_s, pulses, offs_v, geo_v, dft, column, row, lead, image, win, coef, acc
):
    low, high = own_image(
        offs_s, geo_s, count_s, pulses, offs_v, geo_v, dft, column, row, lead, win, coef, acc, ROWS, COLS
    )
    image[:, : COLS // 2] = low
    image[:, COLS // 2 :] = high


def shards(pulses, offsets, geometry, counts):
    rows, cols, width = ROWS, COLS, BINS
    slots = pulses.shape[1]
    constants = [jnp.asarray(t) for t in tables(width, rows, cols)]
    smem = pl.BlockSpec(memory_space=pltpu.SMEM)
    vmem = pl.BlockSpec(memory_space=pltpu.VMEM)
    total = pl.pallas_call(
        image_kernel,
        out_shape=jax.ShapeDtypeStruct((2 * rows, cols), jnp.float32),
        in_specs=[smem] * 3 + [vmem] * 7,
        out_specs=vmem,
        scratch_shapes=[
            pltpu.VMEM((2 * slots, width), jnp.float32),
            pltpu.VMEM((2 * (rows // 8), slots, width), jnp.float32),
            pltpu.VMEM((2 * rows, cols), jnp.float32),
        ],
    )(offsets, geometry, counts, pulses, offsets, geometry, *constants)
    flattened = total.reshape(1, 2 * rows * cols)
    by_pixels = lax.all_to_all(flattened, "sub", split_axis=1, concat_axis=0, tiled=True)
    members = by_pixels.shape[0]
    running = jnp.cumsum(by_pixels, axis=0)
    delayed = jnp.concatenate([jnp.zeros((8, running.shape[1]), jnp.float32), running[:-8]], axis=0)
    frame_rows = (running - delayed) / math.sqrt(8.0)
    magnitude_factor = jnp.sqrt(jnp.arange(1, members + 1, dtype=jnp.int32).astype(jnp.float32))
    cumulative_rows = running / magnitude_factor[:, None]
    frames_back, cumulative_back = (
        lax.all_to_all(frame_rows, "sub", split_axis=0, concat_axis=1, tiled=True),
        lax.all_to_all(cumulative_rows, "sub", split_axis=0, concat_axis=1, tiled=True),
    )
    return (
        frames_back.reshape(1, 2, rows, cols),
        cumulative_back.reshape(1, 2, rows, cols),
    )


def solution(mesh):
    return jax.shard_map(
        shards,
        mesh=mesh,
        in_specs=(
            P(("win", "sub"), None, None, None),
            P(("win", "sub"), None),
            P(("win", "sub"), None, None),
            P(("win", "sub")),
        ),
        out_specs=(P(("win", "sub"), None, None, None), P(("win", "sub"), None, None, None)),
        check_vma=False,
    )
```

```python
import functools
import math

import jax
import jax.numpy as jnp
import numpy as np
from jax import lax
from jax.experimental import pallas as pl
from jax.experimental.pallas import tpu as pltpu
from jax.sharding import PartitionSpec as P

ROWS = 32
COLS = 512
BINS = 128
GROUP = 4
HIGHEST = lax.Precision.HIGHEST

_N = 4001


def _sine_series():
    u = 0.25 * np.cos(np.pi * (np.arange(_N) + 0.5) / _N)
    basis = np.stack([u ** (2 * k + 1) for k in range(6)], axis=1)
    scale = np.abs(basis).max(axis=0)
    fit = np.linalg.lstsq(basis / scale, np.sin(2.0 * np.pi * u), rcond=None)[0] / scale
    return [float(np.float32(c)) for c in fit]


SINE = _sine_series()


def quarter_sine(u):
    z = u * u
    total = SINE[5]
    for k in (4, 3, 2, 1, 0):
        total = total * z + SINE[k]
    return total * u


def cos_sin(turns):
    r = turns - jnp.round(turns)
    a = jnp.abs(r)
    s = quarter_sine(jnp.minimum(a, 0.5 - a))
    return quarter_sine(0.25 - a), jnp.where(r < 0, -s, s)


def frequency_order(width):
    order = []
    for j in range(width // 16):
        order += [16 * j + 8 + l for l in range(8)] + [16 * j + 7 - l for l in range(8)]
    return np.array(order)


def tables(width, rows, cols):
    order = frequency_order(width)
    g = order - width // 2
    b = np.arange(width)
    angle = 2.0 * np.pi * ((b[:, None] * g[None, :]) % width) / width
    dft = np.concatenate([np.cos(angle), np.sin(angle)], axis=1) / width
    tau = g / width + 0.37
    m = np.arange(1, cols // 2 + 1)
    l = np.arange(8)
    middles = (16 * np.arange(width // 16) + 7.5 - width // 2) / width + 0.37
    side = ((l + 0.5) / width)[:, None] * m[None, :] * 0.05
    middle = middles[:, None] * m[None, :] * 0.05
    row = l[:, None] * tau[None, :] * 0.05
    lead = np.stack([tau, g], axis=0)
    f32 = np.float32
    return (
        dft.astype(f32),
        np.concatenate([side, middle], axis=0).astype(f32),
        row.astype(f32),
        lead.astype(f32),
    )


def fetch_kernel(offs_s, pulses, win):
    slots, width = pulses.shape[1], win.shape[1]
    last = pulses.shape[3] // width - 2
    lanes = lax.broadcasted_iota(jnp.int32, (2, width), 1)

    def fetch(p):
        offset = offs_s[0, p]
        block = jnp.minimum(offset // width, last)
        rest = offset - block * width
        first = pulses[0, p, :, pl.ds(pl.multiple_of(block * width, width), width)]
        second = pulses[0, p, :, pl.ds(pl.multiple_of(block * width + width, width), width)]
        both = jnp.where(
            lanes >= rest, first.astype(jnp.float32), second.astype(jnp.float32)
        )
        win[pl.ds(p, 1), :] = both[0:1]
        win[pl.ds(slots + p, 1), :] = both[1:2]

    def fetch_some(i, _):
        for k in range(8):
            fetch(i * 8 + k)
        return 0

    lax.fori_loop(0, slots // 8, fetch_some, 0)


def own_image(geo_s, count_s, win, offs_v, geo_v, dft, column, row, lead, coef, acc, last, rows, cols):
    slots, width = offs_v.shape[1], dft.shape[0]
    half = cols // 2

    out = jnp.dot(win[...], dft[...], precision=HIGHEST, preferred_element_type=jnp.float32)
    spec_re = out[:slots, :width] + out[slots:, width:]
    spec_im = out[slots:, :width] - out[:slots, width:]

    eye = lax.broadcasted_iota(jnp.int32, (slots, slots), 0) == lax.broadcasted_iota(
        jnp.int32, (slots, slots), 1
    )

    def upright(line):
        return jnp.sum(jnp.where(eye, line, 0.0), axis=1, keepdims=True)

    offset_line = offs_v[...]
    block_line = jnp.minimum(offset_line // width, last)
    rest = upright((offset_line - block_line * width).astype(jnp.float32))
    carrier = upright((37 * offset_line % 100).astype(jnp.float32) / 100.0)
    centre = width / 2.0 + width / 16.0 * upright(geo_v[0])
    slope = 0.05 * upright(geo_v[1])
    tau = lead[0:1, :]
    turned = lead[1:2, :] * rest * (1.0 / width)
    phase = tau * centre
    phase = (phase - jnp.round(phase)) + carrier + (turned - jnp.round(turned))
    live = jnp.where(
        lax.broadcasted_iota(jnp.int32, (slots, 1), 0) < count_s[0], 1.0 / math.sqrt(slots), 0.0
    )
    spec_re = spec_re * live
    spec_im = spec_im * live
    blocks = rows // 8
    for q in range(blocks):
        c, s = cos_sin(phase + tau * slope * float(8 * q - rows // 2))
        coef[2 * q] = spec_re * c - spec_im * s
        coef[2 * q + 1] = spec_re * s + spec_im * c

    acc[...] = jnp.zeros_like(acc)

    def pulse(p):
        cx, sx = cos_sin(row[...] * geo_s[1, 0, p])
        real, imag = [], []
        for q in range(blocks):
            cr = coef[2 * q, pl.ds(p, 1), :]
            ci = coef[2 * q + 1, pl.ds(p, 1), :]
            real.append(cr * cx - ci * sx)
            imag.append(cr * sx + ci * cx)
        left = jnp.concatenate(real + imag, axis=0).astype(jnp.bfloat16)
        cy, sy = cos_sin(column[...] * geo_s[2, 0, p])
        c0, s0 = cy[:8], sy[:8]
        right_c, right_s = [], []
        for j in range(width // 16):
            cm, sm = cy[8 + j : 9 + j], sy[8 + j : 9 + j]
            cc, ss, sc, cs = cm * c0, sm * s0, sm * c0, cm * s0
            right_c += [cc - ss, cc + ss]
            right_s += [sc + cs, sc - cs]
        right = jnp.concatenate(
            [
                jnp.concatenate(right_c, axis=0).astype(jnp.bfloat16),
                jnp.concatenate(right_s, axis=0).astype(jnp.bfloat16),
            ],
            axis=1,
        )
        return left, right

    def step(i, total):
        lefts, rights = [], []
        for k in range(GROUP):
            left, right = pulse(i * GROUP + k)
            total = total + left.astype(jnp.float32)
            lefts.append(left)
            rights.append(right)
        acc[...] += jnp.dot(
            jnp.concatenate(lefts, axis=1),
            jnp.concatenate(rights, axis=0),
            preferred_element_type=jnp.float32,
        )
        return total

    total = lax.fori_loop(
        0, slots // GROUP, step, jnp.zeros((2 * rows, width), jnp.float32)
    )
    zero = jnp.sum(total, axis=1, keepdims=True)
    rc, rs = acc[:rows, :half], acc[:rows, half:]
    ic, is_ = acc[rows:, :half], acc[rows:, half:]
    ahead = jnp.concatenate([rc - is_, rs + ic], axis=0)
    behind = jnp.concatenate([rc + is_, ic - rs], axis=0)
    flip = (
        lax.broadcasted_iota(jnp.int32, (half, half), 0)
        + lax.broadcasted_iota(jnp.int32, (half, half), 1)
        == half - 1
    ).astype(jnp.float32)
    low = jnp.dot(behind, flip, precision=HIGHEST, preferred_element_type=jnp.float32)
    high = pltpu.roll(ahead, 1, 1)
    high = jnp.where(lax.broadcasted_iota(jnp.int32, high.shape, 1) == 0, zero, high)
    return low, high


def kernel(
    members,
    last,
    geo_s,
    count_s,
    win,
    offs_v,
    geo_v,
    dft,
    column,
    row,
    lead,
    frames,
    cumulative,
    coef,
    acc,
    mine,
    shares,
    sums,
    back,
    send_a,
    recv_a,
    send_b,
    recv_b,
):
    me = lax.axis_index("sub")
    flat = members <= 32

    def others(body):
        def go(d, _):
            body(lax.rem(me + d, members))
            return 0

        lax.fori_loop(1, members, go, 0, unroll=flat)

    barrier = pltpu.get_barrier_semaphore()
    others(lambda peer: pl.semaphore_signal(barrier, inc=1, device_id={"sub": peer}))

    rows, cols = ROWS, COLS
    half = cols // 2
    low, high = own_image(
        geo_s, count_s, win, offs_v, geo_v, dft, column, row, lead, coef, acc, last, rows, cols
    )
    tall = 2 * rows
    share = mine.shape[1]
    each = tall // share
    for c in range(cols // 128):
        part = low if c * 128 < half else high
        at = c * 128 % half
        for k in range(each):
            mine[c * each + k] = part[k * share : (k + 1) * share, at : at + 128]
    shares[me] = mine[me]

    pl.semaphore_wait(barrier, members - 1)

    def first(peer):
        return pltpu.make_async_remote_copy(
            src_ref=mine.at[peer],
            dst_ref=shares.at[me],
            send_sem=send_a.at[peer],
            recv_sem=recv_a.at[me],
            device_id={"sub": peer},
        )

    def first_in(peer):
        return pltpu.make_async_remote_copy(
            src_ref=mine.at[peer],
            dst_ref=shares.at[peer],
            send_sem=send_a.at[peer],
            recv_sem=recv_a.at[peer],
            device_id={"sub": peer},
        )

    others(lambda peer: first(peer).start())
    others(lambda peer: first_in(peer).wait_recv())

    running = []
    for s in range(members):
        running.append(shares[s] if s == 0 else running[-1] + shares[s])
        frame = running[s] if s < 8 else running[s] - running[s - 8]
        sums[s, 0] = frame * (1.0 / math.sqrt(8.0))
        sums[s, 1] = running[s] * (1.0 / math.sqrt(s + 1.0))
    back[me] = sums[me]

    def second(peer):
        return pltpu.make_async_remote_copy(
            src_ref=sums.at[peer],
            dst_ref=back.at[me],
            send_sem=send_b.at[peer],
            recv_sem=recv_b.at[me],
            device_id={"sub": peer},
        )

    def second_in(peer):
        return pltpu.make_async_remote_copy(
            src_ref=sums.at[peer],
            dst_ref=back.at[peer],
            send_sem=send_b.at[peer],
            recv_sem=recv_b.at[peer],
            device_id={"sub": peer},
        )

    others(lambda peer: second(peer).start())
    others(lambda peer: first(peer).wait_send())
    others(lambda peer: second_in(peer).wait_recv())
    for j in range(members):
        c, k = j // each, j % each
        at = slice(k * share, (k + 1) * share), slice(c * 128, (c + 1) * 128)
        frames[at] = back[j, 0]
        cumulative[at] = back[j, 1]
    others(lambda peer: second(peer).wait_send())


def shards(pulses, offsets, geometry, counts):
    rows, cols, width = ROWS, COLS, BINS
    slots = pulses.shape[1]
    members = lax.axis_size("sub")
    constants = [jnp.asarray(t) for t in tables(width, rows, cols)]
    track = jnp.transpose(geometry, (1, 0, 2))
    smem = pl.BlockSpec(memory_space=pltpu.SMEM)
    vmem = pl.BlockSpec(memory_space=pltpu.VMEM)
    share = 2 * rows * cols // 128 // members
    whole = jax.ShapeDtypeStruct((2 * rows, cols), jnp.float32)
    dma = pltpu.SemaphoreType.DMA((members,))
    win = pl.pallas_call(
        fetch_kernel,
        out_shape=jax.ShapeDtypeStruct((2 * slots, width), jnp.float32),
        in_specs=[smem, vmem],
        out_specs=vmem,
    )(offsets, pulses)
    last = pulses.shape[3] // width - 2
    frames, cumulative = pl.pallas_call(
        functools.partial(kernel, members, last),
        out_shape=(whole, whole),
        in_specs=[smem] * 2 + [vmem] * 7,
        out_specs=(vmem, vmem),
        scratch_shapes=[
            pltpu.VMEM((2 * (rows // 8), slots, width), jnp.float32),
            pltpu.VMEM((2 * rows, cols), jnp.float32),
            pltpu.VMEM((members, share, 128), jnp.float32),
            pltpu.VMEM((members, share, 128), jnp.float32),
            pltpu.VMEM((members, 2, share, 128), jnp.float32),
            pltpu.VMEM((members, 2, share, 128), jnp.float32),
            dma,
            dma,
            dma,
            dma,
        ],
        compiler_params=pltpu.CompilerParams(collective_id=0, has_side_effects=True),
    )(track, counts, win, offsets, track, *constants)
    return frames.reshape(1, 2, rows, cols), cumulative.reshape(1, 2, rows, cols)


def solution(mesh):
    return jax.shard_map(
        shards,
        mesh=mesh,
        in_specs=(
            P(("win", "sub"), None, None, None),
            P(("win", "sub"), None),
            P(("win", "sub"), None, None),
            P(("win", "sub")),
        ),
        out_specs=(P(("win", "sub"), None, None, None), P(("win", "sub"), None, None, None)),
        check_vma=False,
    )
```

```python
import functools
import math

import jax
import jax.numpy as jnp
import numpy as np
from jax import lax
from jax.experimental import pallas as pl
from jax.experimental.pallas import tpu as pltpu
from jax.sharding import PartitionSpec as P

ROWS = 32
COLS = 512
BINS = 128
GROUP = 4
HIGHEST = lax.Precision.HIGHEST

_N = 4001


def _sine_series():
    u = 0.25 * np.cos(np.pi * (np.arange(_N) + 0.5) / _N)
    basis = np.stack([u ** (2 * k + 1) for k in range(6)], axis=1)
    scale = np.abs(basis).max(axis=0)
    fit = np.linalg.lstsq(basis / scale, np.sin(2.0 * np.pi * u), rcond=None)[0] / scale
    return [float(np.float32(c)) for c in fit]


SINE = _sine_series()


def quarter_sine(u):
    z = u * u
    total = SINE[5]
    for k in (4, 3, 2, 1, 0):
        total = total * z + SINE[k]
    return total * u


def cos_sin(turns):
    r = turns - jnp.round(turns)
    a = jnp.abs(r)
    s = quarter_sine(jnp.minimum(a, 0.5 - a))
    return quarter_sine(0.25 - a), jnp.where(r < 0, -s, s)


def frequency_order(width):
    order = []
    for j in range(width // 16):
        order += [16 * j + 8 + l for l in range(8)] + [16 * j + 7 - l for l in range(8)]
    return np.array(order)


def tables(width, rows, cols):
    order = frequency_order(width)
    g = order - width // 2
    b = np.arange(width)
    angle = 2.0 * np.pi * ((b[:, None] * g[None, :]) % width) / width
    dft = np.concatenate([np.cos(angle), np.sin(angle)], axis=1) / width
    tau = g / width + 0.37
    m = np.arange(1, cols // 2 + 1)
    l = np.arange(8)
    middles = (16 * np.arange(width // 16) + 7.5 - width // 2) / width + 0.37
    side = ((l + 0.5) / width)[:, None] * m[None, :] * 0.05
    middle = middles[:, None] * m[None, :] * 0.05
    row = l[:, None] * tau[None, :] * 0.05
    lead = np.stack([tau, g], axis=0)
    f32 = np.float32
    return (
        dft.astype(f32),
        np.concatenate([side, middle], axis=0).astype(f32),
        row.astype(f32),
        lead.astype(f32),
    )


def fetch_kernel(offs_s, pulses, win):
    slots, width = pulses.shape[1], win.shape[1]
    last = pulses.shape[3] // width - 2
    lanes = lax.broadcasted_iota(jnp.int32, (2, width), 1)

    def fetch(p):
        offset = offs_s[0, p]
        block = jnp.minimum(offset // width, last)
        rest = offset - block * width
        first = pulses[0, p, :, pl.ds(pl.multiple_of(block * width, width), width)]
        second = pulses[0, p, :, pl.ds(pl.multiple_of(block * width + width, width), width)]
        both = jnp.where(
            lanes >= rest, first.astype(jnp.float32), second.astype(jnp.float32)
        )
        win[pl.ds(p, 1), :] = both[0:1]
        win[pl.ds(slots + p, 1), :] = both[1:2]

    def fetch_some(i, _):
        for k in range(8):
            fetch(i * 8 + k)
        return 0

    lax.fori_loop(0, slots // 8, fetch_some, 0)


def prepare(count_s, win, offs_v, geo_v, dft, lead, coef, last, rows):
    slots, width = offs_v.shape[1], dft.shape[0]

    out = jnp.dot(win[...], dft[...], precision=HIGHEST, preferred_element_type=jnp.float32)
    spec_re = out[:slots, :width] + out[slots:, width:]
    spec_im = out[slots:, :width] - out[:slots, width:]

    eye = lax.broadcasted_iota(jnp.int32, (slots, slots), 0) == lax.broadcasted_iota(
        jnp.int32, (slots, slots), 1
    )

    def upright(line):
        return jnp.sum(jnp.where(eye, line, 0.0), axis=1, keepdims=True)

    offset_line = offs_v[...]
    block_line = jnp.minimum(offset_line // width, last)
    rest = upright((offset_line - block_line * width).astype(jnp.float32))
    carrier = upright((37 * offset_line % 100).astype(jnp.float32) / 100.0)
    centre = width / 2.0 + width / 16.0 * upright(geo_v[0])
    slope = 0.05 * upright(geo_v[1])
    tau = lead[0:1, :]
    turned = lead[1:2, :] * rest * (1.0 / width)
    phase = tau * centre
    phase = (phase - jnp.round(phase)) + carrier + (turned - jnp.round(turned))
    live = jnp.where(
        lax.broadcasted_iota(jnp.int32, (slots, 1), 0) < count_s[0], 1.0 / math.sqrt(slots), 0.0
    )
    spec_re = spec_re * live
    spec_im = spec_im * live
    blocks = rows // 8
    for q in range(blocks):
        c, s = cos_sin(phase + tau * slope * float(8 * q - rows // 2))
        coef[2 * q] = spec_re * c - spec_im * s
        coef[2 * q + 1] = spec_re * s + spec_im * c


def lefts_of(p, geo_s, row, coef, rows):
    blocks = rows // 8
    cx, sx = cos_sin(row[...] * geo_s[1, 0, p])
    real, imag = [], []
    for q in range(blocks):
        cr = coef[2 * q, pl.ds(p, 1), :]
        ci = coef[2 * q + 1, pl.ds(p, 1), :]
        real.append(cr * cx - ci * sx)
        imag.append(cr * sx + ci * cx)
    return jnp.concatenate(real + imag, axis=0).astype(jnp.bfloat16)


def right_of(p, geo_s, column, at, width):
    cy, sy = cos_sin(column[:, at : at + 128] * geo_s[2, 0, p])
    c0, s0 = cy[:8], sy[:8]
    right_c, right_s = [], []
    for j in range(width // 16):
        cm, sm = cy[8 + j : 9 + j], sy[8 + j : 9 + j]
        cc, ss, sc, cs = cm * c0, sm * s0, sm * c0, cm * s0
        right_c += [cc - ss, cc + ss]
        right_s += [sc + cs, sc - cs]
    return jnp.concatenate(
        [
            jnp.concatenate(right_c, axis=0).astype(jnp.bfloat16),
            jnp.concatenate(right_s, axis=0).astype(jnp.bfloat16),
        ],
        axis=1,
    )


def one_pass(h, geo_s, column, row, coef, left_all, acc, slots, width, rows):
    acc[...] = jnp.zeros_like(acc)

    def step(i, total):
        rights = []
        for k in range(GROUP):
            p = i * GROUP + k
            if h == 0:
                left = lefts_of(p, geo_s, row, coef, rows)
                left_all[i, :, k * width : (k + 1) * width] = left
                total = total + left.astype(jnp.float32)
            rights.append(right_of(p, geo_s, column, 128 * h, width))
        acc[...] += jnp.dot(
            left_all[i],
            jnp.concatenate(rights, axis=0),
            preferred_element_type=jnp.float32,
        )
        return total

    if h == 0:
        total = lax.fori_loop(
            0, slots // GROUP, step, jnp.zeros((2 * rows, width), jnp.float32)
        )
        zero = jnp.sum(total, axis=1, keepdims=True)
    else:
        lax.fori_loop(0, slots // GROUP, step, 0)
        zero = None
    rc, rs = acc[:rows, :128], acc[:rows, 128:]
    ic, is_ = acc[rows:, :128], acc[rows:, 128:]
    ahead = jnp.concatenate([rc - is_, rs + ic], axis=0)
    behind = jnp.concatenate([rc + is_, ic - rs], axis=0)
    flip = (
        lax.broadcasted_iota(jnp.int32, (128, 128), 0)
        + lax.broadcasted_iota(jnp.int32, (128, 128), 1)
        == 127
    ).astype(jnp.float32)
    low = jnp.dot(behind, flip, precision=HIGHEST, preferred_element_type=jnp.float32)
    return low, ahead, zero


def kernel(
    members,
    last,
    geo_s,
    count_s,
    win,
    offs_v,
    geo_v,
    dft,
    column,
    row,
    lead,
    frames,
    cumulative,
    coef,
    left_all,
    acc,
    mine,
    shares,
    sums,
    back,
    send_a,
    recv_a,
    send_b,
    recv_b,
):
    me = lax.axis_index("sub")
    order = sorted(range(1, members), key=lambda d: abs(2 * d - members))

    def others(body):
        if members <= 32:
            for d in order:
                body(lax.rem(me + d, members))
            return

        def go(d, _):
            body(lax.rem(me + d, members))
            return 0

        lax.fori_loop(1, members, go, 0)

    barrier = pltpu.get_barrier_semaphore()
    others(lambda peer: pl.semaphore_signal(barrier, inc=1, device_id={"sub": peer}))

    rows, cols, width, slots = ROWS, COLS, BINS, offs_v.shape[1]
    passes = cols // 256
    tall = 2 * rows
    share = mine.shape[2]
    each = tall // share

    def copy_of(source, target, sends, recvs, h, peer, owner):
        return pltpu.make_async_remote_copy(
            src_ref=source.at[h, peer],
            dst_ref=target.at[h, owner],
            send_sem=sends.at[h, peer],
            recv_sem=recvs.at[h, owner],
            device_id={"sub": peer},
        )

    def first(h, peer, owner):
        return copy_of(mine, shares, send_a, recv_a, h, peer, owner)

    def second(h, peer, owner):
        return copy_of(sums, back, send_b, recv_b, h, peer, owner)

    prepare(count_s, win, offs_v, geo_v, dft, lead, coef, last, rows)
    before = None
    for h in range(passes):
        low, ahead, zero = one_pass(
            h, geo_s, column, row, coef, left_all, acc, slots, width, rows
        )
        high = pltpu.roll(ahead, 1, 1)
        edge = lax.broadcasted_iota(jnp.int32, high.shape, 1) == 0
        high = jnp.where(edge, zero if h == 0 else before, high)
        before = pltpu.roll(ahead, 1, 1)
        for k in range(each):
            mine[h, k] = low[k * share : (k + 1) * share]
            mine[h, each + k] = high[k * share : (k + 1) * share]
        shares[h, me] = mine[h, me]
        if h == 0:
            pl.semaphore_wait(barrier, members - 1)
        others(lambda peer: first(h, peer, me).start())

    for h in range(passes):
        others(lambda peer: first(h, peer, peer).wait_recv())
        running = []
        for s in range(members):
            running.append(shares[h, s] if s == 0 else running[-1] + shares[h, s])
            frame = running[s] if s < 8 else running[s] - running[s - 8]
            sums[h, s, 0] = frame * (1.0 / math.sqrt(8.0))
            sums[h, s, 1] = running[s] * (1.0 / math.sqrt(s + 1.0))
        back[h, me] = sums[h, me]
        others(lambda peer: second(h, peer, me).start())

    for h in range(passes):
        others(lambda peer: first(h, peer, me).wait_send())
    for h in range(passes):
        others(lambda peer: second(h, peer, peer).wait_recv())
        for j in range(members):
            k = j % each
            c = passes - 1 - h if j < each else passes + h
            at = slice(k * share, (k + 1) * share), slice(c * 128, (c + 1) * 128)
            frames[at] = back[h, j, 0]
            cumulative[at] = back[h, j, 1]
    for h in range(passes):
        others(lambda peer: second(h, peer, me).wait_send())


def shards(pulses, offsets, geometry, counts):
    rows, cols, width = ROWS, COLS, BINS
    slots = pulses.shape[1]
    members = lax.axis_size("sub")
    constants = [jnp.asarray(t) for t in tables(width, rows, cols)]
    track = jnp.transpose(geometry, (1, 0, 2))
    smem = pl.BlockSpec(memory_space=pltpu.SMEM)
    vmem = pl.BlockSpec(memory_space=pltpu.VMEM)
    passes = cols // 256
    share = 4 * rows // members
    whole = jax.ShapeDtypeStruct((2 * rows, cols), jnp.float32)
    dma = pltpu.SemaphoreType.DMA((passes, members))
    win = pl.pallas_call(
        fetch_kernel,
        out_shape=jax.ShapeDtypeStruct((2 * slots, width), jnp.float32),
        in_specs=[smem, vmem],
        out_specs=vmem,
        compiler_params=pltpu.CompilerParams(vmem_limit_bytes=16 * 2**20),
    )(offsets, pulses)
    last = pulses.shape[3] // width - 2
    frames, cumulative = pl.pallas_call(
        functools.partial(kernel, members, last),
        out_shape=(whole, whole),
        in_specs=[smem] * 2 + [vmem] * 7,
        out_specs=(vmem, vmem),
        scratch_shapes=[
            pltpu.VMEM((2 * (rows // 8), slots, width), jnp.float32),
            pltpu.VMEM((slots // GROUP, 2 * rows, GROUP * width), jnp.bfloat16),
            pltpu.VMEM((2 * rows, 256), jnp.float32),
            pltpu.VMEM((passes, members, share, 128), jnp.float32),
            pltpu.VMEM((passes, members, share, 128), jnp.float32),
            pltpu.VMEM((passes, members, 2, share, 128), jnp.float32),
            pltpu.VMEM((passes, members, 2, share, 128), jnp.float32),
            dma,
            dma,
            dma,
            dma,
        ],
        compiler_params=pltpu.CompilerParams(
            collective_id=0, has_side_effects=True, vmem_limit_bytes=16 * 2**20
        ),
    )(track, counts, win, offsets, track, *constants)
    return frames.reshape(1, 2, rows, cols), cumulative.reshape(1, 2, rows, cols)


def solution(mesh):
    return jax.shard_map(
        shards,
        mesh=mesh,
        in_specs=(
            P(("win", "sub"), None, None, None),
            P(("win", "sub"), None),
            P(("win", "sub"), None, None),
            P(("win", "sub")),
        ),
        out_specs=(P(("win", "sub"), None, None, None), P(("win", "sub"), None, None, None)),
        check_vma=False,
    )
```

```python
import functools
import math

import jax
import jax.numpy as jnp
import numpy as np
from jax import lax
from jax.experimental import pallas as pl
from jax.experimental.pallas import tpu as pltpu
from jax.sharding import PartitionSpec as P

ROWS = 32
COLS = 512
BINS = 128
GROUP = 8
HIGHEST = lax.Precision.HIGHEST

def _series(count, odd):
    r = 0.5 * np.cos(np.pi * (np.arange(4001) + 0.5) / 4001)
    basis = np.stack([r ** (2 * k + odd) for k in range(count)], axis=1)
    scale = np.abs(basis).max(axis=0)
    wave = np.sin(2.0 * np.pi * r) if odd else np.cos(2.0 * np.pi * r)
    fit = np.linalg.lstsq(basis / scale, wave, rcond=None)[0] / scale
    return [float(np.float32(c)) for c in fit]


COSINE = _series(7, 0)
SINE = _series(7, 1)


def horner(z, series):
    total = z * series[-1] + series[-2]
    for c in series[-3::-1]:
        total = total * z + c
    return total


def cos_sin(turns):
    r = turns - jnp.round(turns)
    z = r * r
    return horner(z, COSINE), horner(z, SINE) * r


def frequency_order(width):
    order = []
    for j in range(width // 16):
        order += [16 * j + 8 + l for l in range(8)] + [16 * j + 7 - l for l in range(8)]
    return np.array(order)


def tables(width, rows, cols):
    order = frequency_order(width)
    g = order - width // 2
    b = np.arange(width)
    angle = 2.0 * np.pi * ((b[:, None] * g[None, :]) % width) / width
    dft = np.concatenate([np.cos(angle), np.sin(angle)], axis=1) / width
    tau = g / width + 0.37
    m = np.arange(1, 129)
    l = np.arange(8)
    middles = (16 * np.arange(width // 16) + 7.5 - width // 2) / width + 0.37
    side = ((l + 0.5) / width)[:, None] * m[None, :] * 0.05
    middle = middles[:, None] * m[None, :] * 0.05
    row = l[:, None] * tau[None, :] * 0.05
    lead = np.stack([tau, g], axis=0)
    f32 = np.float32
    return (
        dft.astype(f32),
        np.concatenate([side, middle], axis=0).astype(f32),
        row.astype(f32),
        lead.astype(f32),
    )


def fetch_kernel(offs_s, pulses, win):
    slots, width = pulses.shape[1], win.shape[1]
    last = pulses.shape[3] // width - 2
    lanes = lax.broadcasted_iota(jnp.int32, (2, width), 1)

    def fetch(p):
        offset = offs_s[0, p]
        block = jnp.minimum(offset // width, last)
        rest = offset - block * width
        first = pulses[0, p, :, pl.ds(pl.multiple_of(block * width, width), width)]
        second = pulses[0, p, :, pl.ds(pl.multiple_of(block * width + width, width), width)]
        both = jnp.where(
            lanes >= rest, first.astype(jnp.float32), second.astype(jnp.float32)
        )
        win[pl.ds(p, 1), :] = both[0:1]
        win[pl.ds(slots + p, 1), :] = both[1:2]

    def fetch_some(i, _):
        for k in range(8):
            fetch(i * 8 + k)
        return 0

    lax.fori_loop(0, slots // 8, fetch_some, 0)


def prepare(count_s, win, offs_v, geo_v, dft, lead, coef, last, rows):
    slots, width = offs_v.shape[1], dft.shape[0]

    out = jnp.dot(win[...], dft[...], precision=HIGHEST, preferred_element_type=jnp.float32)
    spec_re = out[:slots, :width] + out[slots:, width:]
    spec_im = out[slots:, :width] - out[:slots, width:]

    eye = lax.broadcasted_iota(jnp.int32, (slots, slots), 0) == lax.broadcasted_iota(
        jnp.int32, (slots, slots), 1
    )

    def upright(line):
        return jnp.sum(jnp.where(eye, line, 0.0), axis=1, keepdims=True)

    offset_line = offs_v[...]
    block_line = jnp.minimum(offset_line // width, last)
    rest = upright((offset_line - block_line * width).astype(jnp.float32))
    carrier = upright((37 * offset_line % 100).astype(jnp.float32) / 100.0)
    centre = width / 2.0 + width / 16.0 * upright(geo_v[0])
    slope = 0.05 * upright(geo_v[1])
    tau = lead[0:1, :]
    turned = lead[1:2, :] * rest * (1.0 / width)
    phase = tau * centre
    phase = (phase - jnp.round(phase)) + carrier + (turned - jnp.round(turned))
    live = jnp.where(
        lax.broadcasted_iota(jnp.int32, (slots, 1), 0) < count_s[0], 1.0 / math.sqrt(slots), 0.0
    )
    spec_re = spec_re * live
    spec_im = spec_im * live
    blocks = rows // 8
    for q in range(blocks):
        c, s = cos_sin(phase + tau * slope * float(8 * q - rows // 2))
        coef[2 * q] = spec_re * c - spec_im * s
        coef[2 * q + 1] = spec_re * s + spec_im * c


def lefts_of(p, geo_s, row, coef, rows):
    blocks = rows // 8
    cx, sx = cos_sin(row[...] * geo_s[1, 0, p])
    real, imag = [], []
    for q in range(blocks):
        cr = coef[2 * q, pl.ds(p, 1), :]
        ci = coef[2 * q + 1, pl.ds(p, 1), :]
        real.append(cr * cx - ci * sx)
        imag.append(cr * sx + ci * cx)
    return jnp.concatenate(real + imag, axis=0).astype(jnp.bfloat16)


def right_of(h, p, geo_s, column, waves, width):
    if h == 0:
        cy, sy = cos_sin(column[...] * geo_s[2, 0, p])
    else:
        cy, sy = waves[0, p], waves[1, p]
        ce, se = waves[2, p], waves[3, p]
        cy, sy = cy * ce - sy * se, sy * ce + cy * se
    waves[0, p], waves[1, p] = cy, sy
    if h == 0:
        waves[2, p] = jnp.broadcast_to(cy[:, 127:128], cy.shape)
        waves[3, p] = jnp.broadcast_to(sy[:, 127:128], sy.shape)
    c0, s0 = cy[:8], sy[:8]
    right_c, right_s = [], []
    for j in range(width // 16):
        cm, sm = cy[8 + j : 9 + j], sy[8 + j : 9 + j]
        cc, ss, sc, cs = cm * c0, sm * s0, sm * c0, cm * s0
        right_c += [cc - ss, cc + ss]
        right_s += [sc + cs, sc - cs]
    return jnp.concatenate(
        [
            jnp.concatenate(right_c, axis=0).astype(jnp.bfloat16),
            jnp.concatenate(right_s, axis=0).astype(jnp.bfloat16),
        ],
        axis=1,
    )


def one_pass(h, geo_s, column, row, coef, left_all, waves, acc, zeros, slots, width, rows):
    acc[...] = jnp.zeros_like(acc)
    if h == 0:
        zeros[...] = jnp.zeros_like(zeros)

    def step(i, _):
        lefts, rights = [], []
        for k in range(GROUP):
            p = i * GROUP + k
            if h == 0:
                lefts.append(lefts_of(p, geo_s, row, coef, rows))
            rights.append(right_of(h, p, geo_s, column, waves, width))
        if h == 0:
            left = jnp.concatenate(lefts, axis=1)
            left_all[i] = left
            added = zeros[...]
            for left_one in lefts:
                added = added + left_one.astype(jnp.float32)
            zeros[...] = added
        else:
            left = left_all[i]
        acc[...] += jnp.dot(
            left, jnp.concatenate(rights, axis=0), preferred_element_type=jnp.float32
        )
        return 0

    lax.fori_loop(0, slots // GROUP, step, 0)
    zero = jnp.sum(zeros[...], axis=1, keepdims=True) if h == 0 else None
    rc, rs = acc[:rows, :128], acc[:rows, 128:]
    ic, is_ = acc[rows:, :128], acc[rows:, 128:]
    ahead = jnp.concatenate([rc - is_, rs + ic], axis=0)
    behind = jnp.concatenate([rc + is_, ic - rs], axis=0)
    flip = (
        lax.broadcasted_iota(jnp.int32, (128, 128), 0)
        + lax.broadcasted_iota(jnp.int32, (128, 128), 1)
        == 127
    ).astype(jnp.float32)
    low = jnp.dot(behind, flip, precision=HIGHEST, preferred_element_type=jnp.float32)
    return low, ahead, zero


def kernel(
    members,
    last,
    geo_s,
    count_s,
    win,
    offs_v,
    geo_v,
    dft,
    column,
    row,
    lead,
    frames,
    cumulative,
    coef,
    left_all,
    waves,
    acc,
    zeros,
    mine,
    shares,
    sums,
    back,
    send_a,
    recv_a,
    send_b,
    recv_b,
):
    me = lax.axis_index("sub")
    order = sorted(range(1, members), key=lambda d: abs(2 * d - members))

    def others(body):
        if members <= 32:
            for d in order:
                body(lax.rem(me + d, members))
            return

        def go(d, _):
            body(lax.rem(me + d, members))
            return 0

        lax.fori_loop(1, members, go, 0)

    barrier = pltpu.get_barrier_semaphore()
    others(lambda peer: pl.semaphore_signal(barrier, inc=1, device_id={"sub": peer}))

    rows, cols, width, slots = ROWS, COLS, BINS, offs_v.shape[1]
    passes = cols // 256
    tall = 2 * rows
    share = mine.shape[2]
    each = tall // share

    def copy_of(source, target, sends, recvs, h, peer, owner):
        return pltpu.make_async_remote_copy(
            src_ref=source.at[h, peer],
            dst_ref=target.at[h, owner],
            send_sem=sends.at[h, peer],
            recv_sem=recvs.at[h, owner],
            device_id={"sub": peer},
        )

    def first(h, peer, owner):
        return copy_of(mine, shares, send_a, recv_a, h, peer, owner)

    def second(h, peer, owner):
        return copy_of(sums, back, send_b, recv_b, h, peer, owner)

    prepare(count_s, win, offs_v, geo_v, dft, lead, coef, last, rows)
    before = None
    for h in range(passes):
        low, ahead, zero = one_pass(
            h, geo_s, column, row, coef, left_all, waves, acc, zeros, slots, width, rows
        )
        high = pltpu.roll(ahead, 1, 1)
        edge = lax.broadcasted_iota(jnp.int32, high.shape, 1) == 0
        high = jnp.where(edge, zero if h == 0 else before, high)
        before = pltpu.roll(ahead, 1, 1)
        for k in range(each):
            mine[h, k] = low[k * share : (k + 1) * share]
            mine[h, each + k] = high[k * share : (k + 1) * share]
        shares[h, me] = mine[h, me]
        if h == 0:
            pl.semaphore_wait(barrier, members - 1)
        others(lambda peer: first(h, peer, me).start())

    for h in range(passes):
        others(lambda peer: first(h, peer, peer).wait_recv())
        running = []
        for s in range(members):
            running.append(shares[h, s] if s == 0 else running[-1] + shares[h, s])
            frame = running[s] if s < 8 else running[s] - running[s - 8]
            sums[h, s, 0] = frame * (1.0 / math.sqrt(8.0))
            sums[h, s, 1] = running[s] * (1.0 / math.sqrt(s + 1.0))
        back[h, me] = sums[h, me]
        others(lambda peer: second(h, peer, me).start())

    for h in range(passes):
        others(lambda peer: first(h, peer, me).wait_send())
    for h in range(passes):
        others(lambda peer: second(h, peer, peer).wait_recv())
        for j in range(members):
            k = j % each
            c = passes - 1 - h if j < each else passes + h
            at = slice(k * share, (k + 1) * share), slice(c * 128, (c + 1) * 128)
            frames[at] = back[h, j, 0]
            cumulative[at] = back[h, j, 1]
    for h in range(passes):
        others(lambda peer: second(h, peer, me).wait_send())


def shards(pulses, offsets, geometry, counts):
    rows, cols, width = ROWS, COLS, BINS
    slots = pulses.shape[1]
    members = lax.axis_size("sub")
    constants = [jnp.asarray(t) for t in tables(width, rows, cols)]
    track = jnp.transpose(geometry, (1, 0, 2))
    smem = pl.BlockSpec(memory_space=pltpu.SMEM)
    vmem = pl.BlockSpec(memory_space=pltpu.VMEM)
    passes = cols // 256
    share = 4 * rows // members
    whole = jax.ShapeDtypeStruct((2 * rows, cols), jnp.float32)
    dma = pltpu.SemaphoreType.DMA((passes, members))
    win = pl.pallas_call(
        fetch_kernel,
        out_shape=jax.ShapeDtypeStruct((2 * slots, width), jnp.float32),
        in_specs=[smem, vmem],
        out_specs=vmem,
        compiler_params=pltpu.CompilerParams(vmem_limit_bytes=16 * 2**20),
    )(offsets, pulses)
    last = pulses.shape[3] // width - 2
    frames, cumulative = pl.pallas_call(
        functools.partial(kernel, members, last),
        out_shape=(whole, whole),
        in_specs=[smem] * 2 + [vmem] * 7,
        out_specs=(vmem, vmem),
        scratch_shapes=[
            pltpu.VMEM((2 * (rows // 8), slots, width), jnp.float32),
            pltpu.VMEM((slots // GROUP, 2 * rows, GROUP * width), jnp.bfloat16),
            pltpu.VMEM((4, slots, 8 + width // 16, 128), jnp.float32),
            pltpu.VMEM((2 * rows, 256), jnp.float32),
            pltpu.VMEM((2 * rows, width), jnp.float32),
            pltpu.VMEM((passes, members, share, 128), jnp.float32),
            pltpu.VMEM((passes, members, share, 128), jnp.float32),
            pltpu.VMEM((passes, members, 2, share, 128), jnp.float32),
            pltpu.VMEM((passes, members, 2, share, 128), jnp.float32),
            dma,
            dma,
            dma,
            dma,
        ],
        compiler_params=pltpu.CompilerParams(
            collective_id=0, has_side_effects=True, vmem_limit_bytes=16 * 2**20
        ),
    )(track, counts, win, offsets, track, *constants)
    return frames.reshape(1, 2, rows, cols), cumulative.reshape(1, 2, rows, cols)


def solution(mesh):
    return jax.shard_map(
        shards,
        mesh=mesh,
        in_specs=(
            P(("win", "sub"), None, None, None),
            P(("win", "sub"), None),
            P(("win", "sub"), None, None),
            P(("win", "sub")),
        ),
        out_specs=(P(("win", "sub"), None, None, None), P(("win", "sub"), None, None, None)),
        check_vma=False,
    )
```

```python
import functools
import math

import jax
import jax.numpy as jnp
import numpy as np
from jax import lax
from jax.experimental import pallas as pl
from jax.experimental.pallas import tpu as pltpu
from jax.sharding import PartitionSpec as P

ROWS = 32
COLS = 512
BINS = 128
GROUP = 8
HIGHEST = lax.Precision.HIGHEST

def _series(count, odd):
    r = 0.5 * np.cos(np.pi * (np.arange(4001) + 0.5) / 4001)
    basis = np.stack([r ** (2 * k + odd) for k in range(count)], axis=1)
    scale = np.abs(basis).max(axis=0)
    wave = np.sin(2.0 * np.pi * r) if odd else np.cos(2.0 * np.pi * r)
    fit = np.linalg.lstsq(basis / scale, wave, rcond=None)[0] / scale
    return [float(np.float32(c)) for c in fit]


COSINE = _series(7, 0)
SINE = _series(7, 1)


def horner(z, series):
    total = z * series[-1] + series[-2]
    for c in series[-3::-1]:
        total = total * z + c
    return total


def cos_sin(turns):
    r = turns - jnp.round(turns)
    z = r * r
    return horner(z, COSINE), horner(z, SINE) * r


def frequency_order(width):
    order = []
    for j in range(width // 16):
        order += [16 * j + 8 + l for l in range(8)] + [16 * j + 7 - l for l in range(8)]
    return np.array(order)


def tables(width, rows, cols):
    order = frequency_order(width)
    g = order - width // 2
    b = np.arange(width)
    angle = 2.0 * np.pi * ((b[:, None] * g[None, :]) % width) / width
    dft = np.concatenate([np.cos(angle), np.sin(angle)], axis=1) / width
    tau = g / width + 0.37
    m = np.arange(1, 129)
    l = np.arange(8)
    middles = (16 * np.arange(width // 16) + 7.5 - width // 2) / width + 0.37
    side = ((l + 0.5) / width)[:, None] * m[None, :] * 0.05
    middle = middles[:, None] * m[None, :] * 0.05
    row = l[:, None] * tau[None, :] * 0.05
    lead = np.stack([tau, g], axis=0)
    f32 = np.float32
    return (
        dft.astype(f32),
        np.concatenate([side, middle], axis=0).astype(f32),
        row.astype(f32),
        lead.astype(f32),
    )


def fetch_kernel(offs_s, pulses_hbm, win, pulses, arrived):
    slots, width = pulses.shape[1], win.shape[1]
    last = pulses.shape[3] // width - 2
    lanes = lax.broadcasted_iota(jnp.int32, (2, width), 1)

    def fetch(p):
        offset = offs_s[0, p]
        block = jnp.minimum(offset // width, last)
        rest = offset - block * width
        first = pulses[0, p, :, pl.ds(pl.multiple_of(block * width, width), width)]
        second = pulses[0, p, :, pl.ds(pl.multiple_of(block * width + width, width), width)]
        both = jnp.where(
            lanes >= rest, first.astype(jnp.float32), second.astype(jnp.float32)
        )
        win[pl.ds(p, 1), :] = both[0:1]
        win[pl.ds(slots + p, 1), :] = both[1:2]

    parts = arrived.shape[0]
    size = slots // parts

    def part(n):
        at = pl.ds(n * size, size)
        return pltpu.make_async_copy(pulses_hbm.at[:, at], pulses.at[:, at], arrived.at[n])

    for n in range(parts):
        part(n).start()
    for n in range(parts):
        part(n).wait()

        def fetch_some(i, _, n=n):
            for k in range(8):
                fetch(n * size + i * 8 + k)
            return 0

        lax.fori_loop(0, size // 8, fetch_some, 0)


def prepare(count_s, win, offs_v, geo_v, dft, lead, coef, last, rows):
    slots, width = offs_v.shape[1], dft.shape[0]

    out = jnp.dot(win[...], dft[...], precision=HIGHEST, preferred_element_type=jnp.float32)
    spec_re = out[:slots, :width] + out[slots:, width:]
    spec_im = out[slots:, :width] - out[:slots, width:]

    eye = lax.broadcasted_iota(jnp.int32, (slots, slots), 0) == lax.broadcasted_iota(
        jnp.int32, (slots, slots), 1
    )

    def upright(line):
        return jnp.sum(jnp.where(eye, line, 0.0), axis=1, keepdims=True)

    offset_line = offs_v[...]
    block_line = jnp.minimum(offset_line // width, last)
    rest = upright((offset_line - block_line * width).astype(jnp.float32))
    carrier = upright((37 * offset_line % 100).astype(jnp.float32) / 100.0)
    centre = width / 2.0 + width / 16.0 * upright(geo_v[0])
    slope = 0.05 * upright(geo_v[1])
    tau = lead[0:1, :]
    turned = lead[1:2, :] * rest * (1.0 / width)
    phase = tau * centre
    phase = (phase - jnp.round(phase)) + carrier + (turned - jnp.round(turned))
    live = jnp.where(
        lax.broadcasted_iota(jnp.int32, (slots, 1), 0) < count_s[0], 1.0 / math.sqrt(slots), 0.0
    )
    spec_re = spec_re * live
    spec_im = spec_im * live
    blocks = rows // 8
    for q in range(blocks):
        c, s = cos_sin(phase + tau * slope * float(8 * q - rows // 2))
        coef[2 * q] = spec_re * c - spec_im * s
        coef[2 * q + 1] = spec_re * s + spec_im * c


def lefts_of(p, geo_s, row, coef, rows):
    blocks = rows // 8
    cx, sx = cos_sin(row[...] * geo_s[1, 0, p])
    real, imag = [], []
    for q in range(blocks):
        cr = coef[2 * q, pl.ds(p, 1), :]
        ci = coef[2 * q + 1, pl.ds(p, 1), :]
        real.append(cr * cx - ci * sx)
        imag.append(cr * sx + ci * cx)
    return jnp.concatenate(real + imag, axis=0).astype(jnp.bfloat16)


def right_of(h, p, geo_s, column, waves, width):
    if h == 0:
        cy, sy = cos_sin(column[...] * geo_s[2, 0, p])
    else:
        cy, sy = waves[0, p], waves[1, p]
        ce, se = waves[2, p], waves[3, p]
        cy, sy = cy * ce - sy * se, sy * ce + cy * se
    waves[0, p], waves[1, p] = cy, sy
    if h == 0:
        waves[2, p] = jnp.broadcast_to(cy[:, 127:128], cy.shape)
        waves[3, p] = jnp.broadcast_to(sy[:, 127:128], sy.shape)
    c0, s0 = cy[:8], sy[:8]
    right_c, right_s = [], []
    for j in range(width // 16):
        cm, sm = cy[8 + j : 9 + j], sy[8 + j : 9 + j]
        cc, ss, sc, cs = cm * c0, sm * s0, sm * c0, cm * s0
        right_c += [cc - ss, cc + ss]
        right_s += [sc + cs, sc - cs]
    return jnp.concatenate(
        [
            jnp.concatenate(right_c, axis=0).astype(jnp.bfloat16),
            jnp.concatenate(right_s, axis=0).astype(jnp.bfloat16),
        ],
        axis=1,
    )


def one_pass(h, geo_s, column, row, coef, left_all, waves, acc, zeros, slots, width, rows):
    acc[...] = jnp.zeros_like(acc)
    if h == 0:
        zeros[...] = jnp.zeros_like(zeros)

    def step(i, _):
        lefts, rights = [], []
        for k in range(GROUP):
            p = i * GROUP + k
            if h == 0:
                lefts.append(lefts_of(p, geo_s, row, coef, rows))
            rights.append(right_of(h, p, geo_s, column, waves, width))
        if h == 0:
            left = jnp.concatenate(lefts, axis=1)
            left_all[i] = left
            added = zeros[...]
            for left_one in lefts:
                added = added + left_one.astype(jnp.float32)
            zeros[...] = added
        else:
            left = left_all[i]
        acc[...] += jnp.dot(
            left, jnp.concatenate(rights, axis=0), preferred_element_type=jnp.float32
        )
        return 0

    lax.fori_loop(0, slots // GROUP, step, 0)
    zero = jnp.sum(zeros[...], axis=1, keepdims=True) if h == 0 else None
    rc, rs = acc[:rows, :128], acc[:rows, 128:]
    ic, is_ = acc[rows:, :128], acc[rows:, 128:]
    ahead = jnp.concatenate([rc - is_, rs + ic], axis=0)
    behind = jnp.concatenate([rc + is_, ic - rs], axis=0)
    flip = (
        lax.broadcasted_iota(jnp.int32, (128, 128), 0)
        + lax.broadcasted_iota(jnp.int32, (128, 128), 1)
        == 127
    ).astype(jnp.float32)
    low = jnp.dot(behind, flip, precision=HIGHEST, preferred_element_type=jnp.float32)
    return low, ahead, zero


def kernel(
    members,
    last,
    geo_s,
    count_s,
    win,
    offs_v,
    geo_v,
    dft,
    column,
    row,
    lead,
    frames,
    cumulative,
    coef,
    left_all,
    waves,
    acc,
    zeros,
    mine,
    shares,
    sums,
    back,
    send_a,
    recv_a,
    send_b,
    recv_b,
):
    me = lax.axis_index("sub")
    order = sorted(range(1, members), key=lambda d: abs(2 * d - members))

    def others(body):
        if members <= 32:
            for d in order:
                body(lax.rem(me + d, members))
            return

        def go(d, _):
            body(lax.rem(me + d, members))
            return 0

        lax.fori_loop(1, members, go, 0)

    barrier = pltpu.get_barrier_semaphore()
    others(lambda peer: pl.semaphore_signal(barrier, inc=1, device_id={"sub": peer}))

    rows, cols, width, slots = ROWS, COLS, BINS, offs_v.shape[1]
    passes = cols // 256
    tall = 2 * rows
    share = mine.shape[2]
    each = tall // share

    def copy_of(source, target, sends, recvs, h, peer, owner):
        return pltpu.make_async_remote_copy(
            src_ref=source.at[h, peer],
            dst_ref=target.at[h, owner],
            send_sem=sends.at[h, peer],
            recv_sem=recvs.at[h, owner],
            device_id={"sub": peer},
        )

    def first(h, peer, owner):
        return copy_of(mine, shares, send_a, recv_a, h, peer, owner)

    def second(h, peer, owner):
        return copy_of(sums, back, send_b, recv_b, h, peer, owner)

    prepare(count_s, win, offs_v, geo_v, dft, lead, coef, last, rows)
    before = None
    for h in range(passes):
        low, ahead, zero = one_pass(
            h, geo_s, column, row, coef, left_all, waves, acc, zeros, slots, width, rows
        )
        high = pltpu.roll(ahead, 1, 1)
        edge = lax.broadcasted_iota(jnp.int32, high.shape, 1) == 0
        high = jnp.where(edge, zero if h == 0 else before, high)
        before = pltpu.roll(ahead, 1, 1)
        for k in range(each):
            mine[h, k] = low[k * share : (k + 1) * share]
            mine[h, each + k] = high[k * share : (k + 1) * share]
        shares[h, me] = mine[h, me]
        if h == 0:
            pl.semaphore_wait(barrier, members - 1)
        others(lambda peer: first(h, peer, me).start())

    for h in range(passes):
        others(lambda peer: first(h, peer, peer).wait_recv())
        running = []
        for s in range(members):
            running.append(shares[h, s] if s == 0 else running[-1] + shares[h, s])
            frame = running[s] if s < 8 else running[s] - running[s - 8]
            sums[h, s, 0] = frame * (1.0 / math.sqrt(8.0))
            sums[h, s, 1] = running[s] * (1.0 / math.sqrt(s + 1.0))
        back[h, me] = sums[h, me]
        others(lambda peer: second(h, peer, me).start())

    for h in range(passes):
        others(lambda peer: first(h, peer, me).wait_send())
    for h in range(passes):
        others(lambda peer: second(h, peer, peer).wait_recv())
        for j in range(members):
            k = j % each
            c = passes - 1 - h if j < each else passes + h
            at = slice(k * share, (k + 1) * share), slice(c * 128, (c + 1) * 128)
            frames[at] = back[h, j, 0]
            cumulative[at] = back[h, j, 1]
    for h in range(passes):
        others(lambda peer: second(h, peer, me).wait_send())


def shards(pulses, offsets, geometry, counts):
    rows, cols, width = ROWS, COLS, BINS
    slots = pulses.shape[1]
    members = lax.axis_size("sub")
    constants = [jnp.asarray(t) for t in tables(width, rows, cols)]
    track = jnp.transpose(geometry, (1, 0, 2))
    smem = pl.BlockSpec(memory_space=pltpu.SMEM)
    vmem = pl.BlockSpec(memory_space=pltpu.VMEM)
    passes = cols // 256
    share = 4 * rows // members
    whole = jax.ShapeDtypeStruct((2 * rows, cols), jnp.float32)
    dma = pltpu.SemaphoreType.DMA((passes, members))
    win = pl.pallas_call(
        fetch_kernel,
        out_shape=jax.ShapeDtypeStruct((2 * slots, width), jnp.float32),
        in_specs=[smem, pl.BlockSpec(memory_space=pltpu.HBM)],
        out_specs=vmem,
        scratch_shapes=[
            pltpu.VMEM(pulses.shape, pulses.dtype),
            pltpu.SemaphoreType.DMA((math.gcd(slots // 8, 5),)),
        ],
        compiler_params=pltpu.CompilerParams(vmem_limit_bytes=16 * 2**20),
    )(offsets, pulses)
    last = pulses.shape[3] // width - 2
    frames, cumulative = pl.pallas_call(
        functools.partial(kernel, members, last),
        out_shape=(whole, whole),
        in_specs=[smem] * 2 + [vmem] * 7,
        out_specs=(vmem, vmem),
        scratch_shapes=[
            pltpu.VMEM((2 * (rows // 8), slots, width), jnp.float32),
            pltpu.VMEM((slots // GROUP, 2 * rows, GROUP * width), jnp.bfloat16),
            pltpu.VMEM((4, slots, 8 + width // 16, 128), jnp.float32),
            pltpu.VMEM((2 * rows, 256), jnp.float32),
            pltpu.VMEM((2 * rows, width), jnp.float32),
            pltpu.VMEM((passes, members, share, 128), jnp.float32),
            pltpu.VMEM((passes, members, share, 128), jnp.float32),
            pltpu.VMEM((passes, members, 2, share, 128), jnp.float32),
            pltpu.VMEM((passes, members, 2, share, 128), jnp.float32),
            dma,
            dma,
            dma,
            dma,
        ],
        compiler_params=pltpu.CompilerParams(
            collective_id=0, has_side_effects=True, vmem_limit_bytes=16 * 2**20
        ),
    )(track, counts, win, offsets, track, *constants)
    return frames.reshape(1, 2, rows, cols), cumulative.reshape(1, 2, rows, cols)


def solution(mesh):
    return jax.shard_map(
        shards,
        mesh=mesh,
        in_specs=(
            P(("win", "sub"), None, None, None),
            P(("win", "sub"), None),
            P(("win", "sub"), None, None),
            P(("win", "sub")),
        ),
        out_specs=(P(("win", "sub"), None, None, None), P(("win", "sub"), None, None, None)),
        check_vma=False,
    )
```

```python
import functools
import math

import jax
import jax.numpy as jnp
import numpy as np
from jax import lax
from jax.experimental import pallas as pl
from jax.experimental.pallas import tpu as pltpu
from jax.sharding import PartitionSpec as P

ROWS = 32
COLS = 512
BINS = 128
GROUP = 8
HIGHEST = lax.Precision.HIGHEST

def _series(count, odd):
    r = 0.5 * np.cos(np.pi * (np.arange(4001) + 0.5) / 4001)
    basis = np.stack([r ** (2 * k + odd) for k in range(count)], axis=1)
    scale = np.abs(basis).max(axis=0)
    wave = np.sin(2.0 * np.pi * r) if odd else np.cos(2.0 * np.pi * r)
    fit = np.linalg.lstsq(basis / scale, wave, rcond=None)[0] / scale
    return [float(np.float32(c)) for c in fit]


COSINE = _series(7, 0)
SINE = _series(7, 1)


def horner(z, series):
    total = z * series[-1] + series[-2]
    for c in series[-3::-1]:
        total = total * z + c
    return total


def cos_sin(turns):
    r = turns - jnp.round(turns)
    z = r * r
    return horner(z, COSINE), horner(z, SINE) * r


def frequency_order(width):
    order = []
    for j in range(width // 16):
        order += [16 * j + 8 + l for l in range(8)] + [16 * j + 7 - l for l in range(8)]
    return np.array(order)


def tables(width, rows, cols):
    order = frequency_order(width)
    g = order - width // 2
    b = np.arange(width)
    angle = 2.0 * np.pi * ((b[:, None] * g[None, :]) % width) / width
    dft = np.concatenate([np.cos(angle), np.sin(angle)], axis=1) / width
    tau = g / width + 0.37
    m = np.arange(1, 129)
    l = np.arange(8)
    middles = (16 * np.arange(width // 16) + 7.5 - width // 2) / width + 0.37
    side = ((l + 0.5) / width)[:, None] * m[None, :] * 0.05
    middle = middles[:, None] * m[None, :] * 0.05
    row = l[:, None] * tau[None, :] * 0.05
    lead = np.stack([tau, g], axis=0)
    f32 = np.float32
    return (
        dft.astype(f32),
        np.concatenate([side, middle], axis=0).astype(f32),
        row.astype(f32),
        lead.astype(f32),
    )


def fetch_kernel(offs_s, pulses_hbm, win, pulses, arrived):
    slots, width = pulses.shape[1], win.shape[1]
    last = pulses.shape[3] // width - 2
    lanes = lax.broadcasted_iota(jnp.int32, (2, width), 1)

    def fetch(p):
        offset = offs_s[0, p]
        block = jnp.minimum(offset // width, last)
        rest = offset - block * width
        first = pulses[0, p, :, pl.ds(pl.multiple_of(block * width, width), width)]
        second = pulses[0, p, :, pl.ds(pl.multiple_of(block * width + width, width), width)]
        both = jnp.where(
            lanes >= rest, first.astype(jnp.float32), second.astype(jnp.float32)
        )
        win[pl.ds(p, 1), :] = both[0:1]
        win[pl.ds(slots + p, 1), :] = both[1:2]

    parts = arrived.shape[0]
    size = slots // parts

    def part(n):
        at = pl.ds(n * size, size)
        return pltpu.make_async_copy(pulses_hbm.at[:, at], pulses.at[:, at], arrived.at[n])

    for n in range(parts):
        part(n).start()
    for n in range(parts):
        part(n).wait()

        def fetch_some(i, _, n=n):
            for k in range(8):
                fetch(n * size + i * 8 + k)
            return 0

        lax.fori_loop(0, size // 8, fetch_some, 0)


def prepare(count_s, win, offs_v, geo_v, dft, lead, coef, last, rows):
    slots, width = offs_v.shape[1], dft.shape[0]

    out = jnp.dot(win[...], dft[...], precision=HIGHEST, preferred_element_type=jnp.float32)
    spec_re = out[:slots, :width] + out[slots:, width:]
    spec_im = out[slots:, :width] - out[:slots, width:]

    eye = lax.broadcasted_iota(jnp.int32, (slots, slots), 0) == lax.broadcasted_iota(
        jnp.int32, (slots, slots), 1
    )

    def upright(line):
        return jnp.sum(jnp.where(eye, line, 0.0), axis=1, keepdims=True)

    offset_line = offs_v[...]
    block_line = jnp.minimum(offset_line // width, last)
    rest = upright((offset_line - block_line * width).astype(jnp.float32))
    carrier = upright((37 * offset_line % 100).astype(jnp.float32) / 100.0)
    centre = width / 2.0 + width / 16.0 * upright(geo_v[0])
    slope = 0.05 * upright(geo_v[1])
    tau = lead[0:1, :]
    turned = lead[1:2, :] * rest * (1.0 / width)
    phase = tau * centre
    phase = (phase - jnp.round(phase)) + carrier + (turned - jnp.round(turned))
    live = jnp.where(
        lax.broadcasted_iota(jnp.int32, (slots, 1), 0) < count_s[0], 1.0 / math.sqrt(slots), 0.0
    )
    spec_re = spec_re * live
    spec_im = spec_im * live
    blocks = rows // 8
    for q in range(blocks):
        c, s = cos_sin(phase + tau * slope * float(8 * q - rows // 2))
        coef[2 * q] = spec_re * c - spec_im * s
        coef[2 * q + 1] = spec_re * s + spec_im * c


def lefts_of(p, geo_s, row, coef, rows):
    blocks = rows // 8
    cx, sx = cos_sin(row[...] * geo_s[1, 0, p])
    real, imag = [], []
    for q in range(blocks):
        cr = coef[2 * q, pl.ds(p, 1), :]
        ci = coef[2 * q + 1, pl.ds(p, 1), :]
        real.append(cr * cx - ci * sx)
        imag.append(cr * sx + ci * cx)
    return jnp.concatenate(real + imag, axis=0).astype(jnp.bfloat16)


def right_of(h, p, geo_s, column, waves, width):
    if h == 0:
        cy, sy = cos_sin(column[...] * geo_s[2, 0, p])
    else:
        cy, sy = waves[0, p], waves[1, p]
        ce, se = waves[2, p], waves[3, p]
        cy, sy = cy * ce - sy * se, sy * ce + cy * se
    waves[0, p], waves[1, p] = cy, sy
    if h == 0:
        waves[2, p] = jnp.broadcast_to(cy[:, 127:128], cy.shape)
        waves[3, p] = jnp.broadcast_to(sy[:, 127:128], sy.shape)
    c0, s0 = cy[:8], sy[:8]
    right_c, right_s = [], []
    for j in range(width // 16):
        cm, sm = cy[8 + j : 9 + j], sy[8 + j : 9 + j]
        cc, ss, sc, cs = cm * c0, sm * s0, sm * c0, cm * s0
        right_c += [cc - ss, cc + ss]
        right_s += [sc + cs, sc - cs]
    return jnp.concatenate(
        [
            jnp.concatenate(right_c, axis=0).astype(jnp.bfloat16),
            jnp.concatenate(right_s, axis=0).astype(jnp.bfloat16),
        ],
        axis=1,
    )


def one_pass(h, geo_s, column, row, coef, left_all, waves, acc, zeros, slots, width, rows):
    acc[...] = jnp.zeros_like(acc)
    if h == 0:
        zeros[...] = jnp.zeros_like(zeros)

    def step(i, _):
        lefts, rights = [], []
        for k in range(GROUP):
            p = i * GROUP + k
            if h == 0:
                lefts.append(lefts_of(p, geo_s, row, coef, rows))
            rights.append(right_of(h, p, geo_s, column, waves, width))
        if h == 0:
            left = jnp.concatenate(lefts, axis=1)
            left_all[i] = left
            added = zeros[...]
            for left_one in lefts:
                added = added + left_one.astype(jnp.float32)
            zeros[...] = added
        else:
            left = left_all[i]
        acc[...] += jnp.dot(
            left, jnp.concatenate(rights, axis=0), preferred_element_type=jnp.float32
        )
        return 0

    lax.fori_loop(0, slots // GROUP, step, 0)
    zero = jnp.sum(zeros[...], axis=1, keepdims=True) if h == 0 else None
    rc, rs = acc[:rows, :128], acc[:rows, 128:]
    ic, is_ = acc[rows:, :128], acc[rows:, 128:]
    ahead = jnp.concatenate([rc - is_, rs + ic], axis=0)
    behind = jnp.concatenate([rc + is_, ic - rs], axis=0)
    flip = (
        lax.broadcasted_iota(jnp.int32, (128, 128), 0)
        + lax.broadcasted_iota(jnp.int32, (128, 128), 1)
        == 127
    ).astype(jnp.float32)
    low = jnp.dot(behind, flip, precision=HIGHEST, preferred_element_type=jnp.float32)
    return low, ahead, zero


def kernel(
    members,
    last,
    geo_s,
    count_s,
    win,
    offs_v,
    geo_v,
    dft,
    column,
    row,
    lead,
    frames,
    cumulative,
    coef,
    left_all,
    waves,
    acc,
    zeros,
    mine,
    shares,
    sums,
    back,
    send_a,
    recv_a,
    send_b,
    recv_b,
):
    me = lax.axis_index("sub")
    order = sorted(range(1, members), key=lambda d: abs(2 * d - members))

    def others(body):
        if members <= 32:
            for d in order:
                body(lax.rem(me + d, members))
            return

        def go(d, _):
            body(lax.rem(me + d, members))
            return 0

        lax.fori_loop(1, members, go, 0)

    barrier = pltpu.get_barrier_semaphore()
    others(lambda peer: pl.semaphore_signal(barrier, inc=1, device_id={"sub": peer}))

    rows, cols, width, slots = ROWS, COLS, BINS, offs_v.shape[1]
    passes = cols // 256
    tall = 2 * rows
    share = mine.shape[2]
    each = tall // share

    def copy_of(source, target, sends, recvs, h, peer, owner):
        return pltpu.make_async_remote_copy(
            src_ref=source.at[h, peer],
            dst_ref=target.at[h, owner],
            send_sem=sends.at[h, peer],
            recv_sem=recvs.at[h, owner],
            device_id={"sub": peer},
        )

    def first(h, peer, owner):
        return copy_of(mine, shares, send_a, recv_a, h, peer, owner)

    def second(h, peer, owner):
        return copy_of(sums, back, send_b, recv_b, h, peer, owner)

    prepare(count_s, win, offs_v, geo_v, dft, lead, coef, last, rows)
    before = None
    for h in range(passes):
        low, ahead, zero = one_pass(
            h, geo_s, column, row, coef, left_all, waves, acc, zeros, slots, width, rows
        )
        high = pltpu.roll(ahead, 1, 1)
        edge = lax.broadcasted_iota(jnp.int32, high.shape, 1) == 0
        high = jnp.where(edge, zero if h == 0 else before, high)
        before = pltpu.roll(ahead, 1, 1)
        for k in range(each):
            mine[h, k] = low[k * share : (k + 1) * share]
            mine[h, each + k] = high[k * share : (k + 1) * share]
        shares[h, me] = mine[h, me]
        if h == 0:
            pl.semaphore_wait(barrier, members - 1)
        others(lambda peer: first(h, peer, me).start())

    for h in range(passes):
        others(lambda peer: first(h, peer, peer).wait_recv())
        running = []
        for s in range(members):
            running.append(shares[h, s] if s == 0 else running[-1] + shares[h, s])
            frame = running[s] if s < 8 else running[s] - running[s - 8]
            sums[h, s, 0] = frame * (1.0 / math.sqrt(8.0))
            sums[h, s, 1] = running[s] * (1.0 / math.sqrt(s + 1.0))
        back[h, me] = sums[h, me]
        others(lambda peer: second(h, peer, me).start())

    for h in range(passes):
        others(lambda peer: first(h, peer, me).wait_send())
    for h in range(passes):
        others(lambda peer: second(h, peer, peer).wait_recv())
        for j in range(members):
            k = j % each
            c = passes - 1 - h if j < each else passes + h
            at = slice(k * share, (k + 1) * share), slice(c * 128, (c + 1) * 128)
            frames[at] = back[h, j, 0]
            cumulative[at] = back[h, j, 1]
    for h in range(passes):
        others(lambda peer: second(h, peer, me).wait_send())


def shards(pulses, offsets, geometry, counts):
    rows, cols, width = ROWS, COLS, BINS
    slots = pulses.shape[1]
    members = lax.axis_size("sub")
    constants = [jnp.asarray(t) for t in tables(width, rows, cols)]
    track = jnp.transpose(geometry, (1, 0, 2))
    smem = pl.BlockSpec(memory_space=pltpu.SMEM)
    vmem = pl.BlockSpec(memory_space=pltpu.VMEM)
    passes = cols // 256
    share = 4 * rows // members
    whole = jax.ShapeDtypeStruct((2 * rows, cols), jnp.float32)
    dma = pltpu.SemaphoreType.DMA((passes, members))
    win = pl.pallas_call(
        fetch_kernel,
        out_shape=jax.ShapeDtypeStruct((2 * slots, width), jnp.float32),
        in_specs=[smem, pl.BlockSpec(memory_space=pltpu.HBM)],
        out_specs=vmem,
        scratch_shapes=[
            pltpu.VMEM(pulses.shape, pulses.dtype),
            pltpu.SemaphoreType.DMA((math.gcd(slots // 8, 5),)),
        ],
    )(offsets, pulses)
    last = pulses.shape[3] // width - 2
    frames, cumulative = pl.pallas_call(
        functools.partial(kernel, members, last),
        out_shape=(whole, whole),
        in_specs=[smem] * 2 + [vmem] * 7,
        out_specs=(vmem, vmem),
        scratch_shapes=[
            pltpu.VMEM((2 * (rows // 8), slots, width), jnp.float32),
            pltpu.VMEM((slots // GROUP, 2 * rows, GROUP * width), jnp.bfloat16),
            pltpu.VMEM((4, slots, 8 + width // 16, 128), jnp.float32),
            pltpu.VMEM((2 * rows, 256), jnp.float32),
            pltpu.VMEM((2 * rows, width), jnp.float32),
            pltpu.VMEM((passes, members, share, 128), jnp.float32),
            pltpu.VMEM((passes, members, share, 128), jnp.float32),
            pltpu.VMEM((passes, members, 2, share, 128), jnp.float32),
            pltpu.VMEM((passes, members, 2, share, 128), jnp.float32),
            dma,
            dma,
            dma,
            dma,
        ],
        compiler_params=pltpu.CompilerParams(
            collective_id=0, has_side_effects=True, vmem_limit_bytes=16 * 2**20
        ),
    )(track, counts, win, offsets, track, *constants)
    return frames.reshape(1, 2, rows, cols), cumulative.reshape(1, 2, rows, cols)


def solution(mesh):
    return jax.shard_map(
        shards,
        mesh=mesh,
        in_specs=(
            P(("win", "sub"), None, None, None),
            P(("win", "sub"), None),
            P(("win", "sub"), None, None),
            P(("win", "sub")),
        ),
        out_specs=(P(("win", "sub"), None, None, None), P(("win", "sub"), None, None, None)),
        check_vma=False,
    )
```

```python
import functools
import math

import jax
import jax.numpy as jnp
import numpy as np
from jax import lax
from jax.experimental import pallas as pl
from jax.experimental.pallas import tpu as pltpu
from jax.sharding import PartitionSpec as P

ROWS = 32
COLS = 512
BINS = 128
GROUP = 16
HIGHEST = lax.Precision.HIGHEST

def _series(count, odd):
    r = 0.5 * np.cos(np.pi * (np.arange(4001) + 0.5) / 4001)
    basis = np.stack([r ** (2 * k + odd) for k in range(count)], axis=1)
    scale = np.abs(basis).max(axis=0)
    wave = np.sin(2.0 * np.pi * r) if odd else np.cos(2.0 * np.pi * r)
    fit = np.linalg.lstsq(basis / scale, wave, rcond=None)[0] / scale
    return [float(np.float32(c)) for c in fit]


COSINE = _series(7, 0)
SINE = _series(7, 1)


def horner(z, series):
    total = z * series[-1] + series[-2]
    for c in series[-3::-1]:
        total = total * z + c
    return total


def cos_sin(turns):
    r = turns - jnp.round(turns)
    z = r * r
    return horner(z, COSINE), horner(z, SINE) * r


def frequency_order(width):
    order = []
    for j in range(width // 16):
        order += [16 * j + 8 + l for l in range(8)] + [16 * j + 7 - l for l in range(8)]
    return np.array(order)


def tables(width, rows, cols):
    order = frequency_order(width)
    g = order - width // 2
    b = np.arange(width)
    angle = 2.0 * np.pi * ((b[:, None] * g[None, :]) % width) / width
    dft = np.concatenate([np.cos(angle), np.sin(angle)], axis=1) / width
    tau = g / width + 0.37
    m = np.arange(1, 129)
    l = np.arange(8)
    middles = (16 * np.arange(width // 16) + 7.5 - width // 2) / width + 0.37
    side = ((l + 0.5) / width)[:, None] * m[None, :] * 0.05
    middle = middles[:, None] * m[None, :] * 0.05
    row = l[:, None] * tau[None, :] * 0.05
    lead = np.stack([tau, g], axis=0)
    f32 = np.float32
    return (
        dft.astype(f32),
        np.concatenate([side, middle], axis=0).astype(f32),
        row.astype(f32),
        lead.astype(f32),
    )


def fetch_kernel(offs_s, pulses, win):
    slots, width = pulses.shape[1], win.shape[1]
    last = pulses.shape[3] // width - 2
    lanes = lax.broadcasted_iota(jnp.int32, (2, width), 1)

    def fetch(p):
        offset = offs_s[0, p]
        block = jnp.minimum(offset // width, last)
        rest = offset - block * width
        first = pulses[0, p, :, pl.ds(pl.multiple_of(block * width, width), width)]
        second = pulses[0, p, :, pl.ds(pl.multiple_of(block * width + width, width), width)]
        both = jnp.where(
            lanes >= rest, first.astype(jnp.float32), second.astype(jnp.float32)
        )
        win[pl.ds(p, 1), :] = both[0:1]
        win[pl.ds(slots + p, 1), :] = both[1:2]

    def fetch_some(i, _):
        for k in range(8):
            fetch(i * 8 + k)
        return 0

    lax.fori_loop(0, slots // 8, fetch_some, 0)


def prepare(count_s, win, offs_v, geo_v, dft, lead, coef, last, rows):
    slots, width = offs_v.shape[1], dft.shape[0]

    out = jnp.dot(win[...], dft[...], precision=HIGHEST, preferred_element_type=jnp.float32)
    spec_re = out[:slots, :width] + out[slots:, width:]
    spec_im = out[slots:, :width] - out[:slots, width:]

    eye = lax.broadcasted_iota(jnp.int32, (slots, slots), 0) == lax.broadcasted_iota(
        jnp.int32, (slots, slots), 1
    )

    def upright(line):
        return jnp.sum(jnp.where(eye, line, 0.0), axis=1, keepdims=True)

    offset_line = offs_v[...]
    block_line = jnp.minimum(offset_line // width, last)
    rest = upright((offset_line - block_line * width).astype(jnp.float32))
    carrier = upright((37 * offset_line % 100).astype(jnp.float32) / 100.0)
    centre = width / 2.0 + width / 16.0 * upright(geo_v[0])
    slope = 0.05 * upright(geo_v[1])
    tau = lead[0:1, :]
    turned = lead[1:2, :] * rest * (1.0 / width)
    phase = tau * centre
    phase = (phase - jnp.round(phase)) + carrier + (turned - jnp.round(turned))
    live = jnp.where(
        lax.broadcasted_iota(jnp.int32, (slots, 1), 0) < count_s[0], 1.0 / math.sqrt(slots), 0.0
    )
    spec_re = spec_re * live
    spec_im = spec_im * live
    blocks = rows // 8
    for q in range(blocks):
        c, s = cos_sin(phase + tau * slope * float(8 * q - rows // 2))
        coef[2 * q] = spec_re * c - spec_im * s
        coef[2 * q + 1] = spec_re * s + spec_im * c


def lefts_of(p, geo_s, row, coef, rows):
    blocks = rows // 8
    cx, sx = cos_sin(row[...] * geo_s[1, 0, p])
    real, imag = [], []
    for q in range(blocks):
        cr = coef[2 * q, pl.ds(p, 1), :]
        ci = coef[2 * q + 1, pl.ds(p, 1), :]
        real.append(cr * cx - ci * sx)
        imag.append(cr * sx + ci * cx)
    return jnp.concatenate(real + imag, axis=0).astype(jnp.bfloat16)


def right_of(h, p, geo_s, column, waves, width):
    if h == 0:
        cy, sy = cos_sin(column[...] * geo_s[2, 0, p])
    else:
        cy, sy = waves[0, p], waves[1, p]
        ce, se = waves[2, p], waves[3, p]
        cy, sy = cy * ce - sy * se, sy * ce + cy * se
    waves[0, p], waves[1, p] = cy, sy
    if h == 0:
        waves[2, p] = jnp.broadcast_to(cy[:, 127:128], cy.shape)
        waves[3, p] = jnp.broadcast_to(sy[:, 127:128], sy.shape)
    c0, s0 = cy[:8], sy[:8]
    right_c, right_s = [], []
    for j in range(width // 16):
        cm, sm = cy[8 + j : 9 + j], sy[8 + j : 9 + j]
        cc, ss, sc, cs = cm * c0, sm * s0, sm * c0, cm * s0
        right_c += [cc - ss, cc + ss]
        right_s += [sc + cs, sc - cs]
    return jnp.concatenate(
        [
            jnp.concatenate(right_c, axis=0).astype(jnp.bfloat16),
            jnp.concatenate(right_s, axis=0).astype(jnp.bfloat16),
        ],
        axis=1,
    )


def one_pass(h, geo_s, column, row, coef, left_all, waves, acc, zeros, slots, width, rows):
    acc[...] = jnp.zeros_like(acc)
    if h == 0:
        zeros[...] = jnp.zeros_like(zeros)

    def step(i, _):
        lefts, rights = [], []
        for k in range(GROUP):
            p = i * GROUP + k
            if h == 0:
                lefts.append(lefts_of(p, geo_s, row, coef, rows))
            rights.append(right_of(h, p, geo_s, column, waves, width))
        if h == 0:
            left = jnp.concatenate(lefts, axis=1)
            left_all[i] = left
            added = zeros[...]
            for left_one in lefts:
                added = added + left_one.astype(jnp.float32)
            zeros[...] = added
        else:
            left = left_all[i]
        acc[...] += jnp.dot(
            left, jnp.concatenate(rights, axis=0), preferred_element_type=jnp.float32
        )
        return 0

    lax.fori_loop(0, slots // GROUP, step, 0)
    zero = jnp.sum(zeros[...], axis=1, keepdims=True) if h == 0 else None
    rc, rs = acc[:rows, :128], acc[:rows, 128:]
    ic, is_ = acc[rows:, :128], acc[rows:, 128:]
    ahead = jnp.concatenate([rc - is_, rs + ic], axis=0)
    behind = jnp.concatenate([rc + is_, ic - rs], axis=0)
    flip = (
        lax.broadcasted_iota(jnp.int32, (128, 128), 0)
        + lax.broadcasted_iota(jnp.int32, (128, 128), 1)
        == 127
    ).astype(jnp.float32)
    low = jnp.dot(behind, flip, precision=HIGHEST, preferred_element_type=jnp.float32)
    return low, ahead, zero


def kernel(
    members,
    last,
    geo_s,
    count_s,
    win,
    offs_v,
    geo_v,
    dft,
    column,
    row,
    lead,
    frames,
    cumulative,
    coef,
    left_all,
    waves,
    acc,
    zeros,
    mine,
    shares,
    sums,
    back,
    send_a,
    recv_a,
    send_b,
    recv_b,
):
    me = lax.axis_index("sub")
    order = sorted(range(1, members), key=lambda d: abs(2 * d - members))

    def others(body):
        if members <= 32:
            for d in order:
                body(lax.rem(me + d, members))
            return

        def go(d, _):
            body(lax.rem(me + d, members))
            return 0

        lax.fori_loop(1, members, go, 0)

    barrier = pltpu.get_barrier_semaphore()
    others(lambda peer: pl.semaphore_signal(barrier, inc=1, device_id={"sub": peer}))

    rows, cols, width, slots = ROWS, COLS, BINS, offs_v.shape[1]
    passes = cols // 256
    tall = 2 * rows
    share = mine.shape[2]
    each = tall // share

    def copy_of(source, target, sends, recvs, h, peer, owner):
        return pltpu.make_async_remote_copy(
            src_ref=source.at[h, peer],
            dst_ref=target.at[h, owner],
            send_sem=sends.at[h, peer],
            recv_sem=recvs.at[h, owner],
            device_id={"sub": peer},
        )

    def first(h, peer, owner):
        return copy_of(mine, shares, send_a, recv_a, h, peer, owner)

    def second(h, peer, owner):
        return copy_of(sums, back, send_b, recv_b, h, peer, owner)

    prepare(count_s, win, offs_v, geo_v, dft, lead, coef, last, rows)
    before = None
    for h in range(passes):
        low, ahead, zero = one_pass(
            h, geo_s, column, row, coef, left_all, waves, acc, zeros, slots, width, rows
        )
        high = pltpu.roll(ahead, 1, 1)
        edge = lax.broadcasted_iota(jnp.int32, high.shape, 1) == 0
        high = jnp.where(edge, zero if h == 0 else before, high)
        before = pltpu.roll(ahead, 1, 1)
        for k in range(each):
            mine[h, k] = low[k * share : (k + 1) * share]
            mine[h, each + k] = high[k * share : (k + 1) * share]
        shares[h, me] = mine[h, me]
        if h == 0:
            pl.semaphore_wait(barrier, members - 1)
        others(lambda peer: first(h, peer, me).start())

    for h in range(passes):
        others(lambda peer: first(h, peer, peer).wait_recv())
        running = []
        for s in range(members):
            running.append(shares[h, s] if s == 0 else running[-1] + shares[h, s])
            frame = running[s] if s < 8 else running[s] - running[s - 8]
            sums[h, s, 0] = frame * (1.0 / math.sqrt(8.0))
            sums[h, s, 1] = running[s] * (1.0 / math.sqrt(s + 1.0))
        back[h, me] = sums[h, me]
        others(lambda peer: second(h, peer, me).start())

    for h in range(passes):
        others(lambda peer: first(h, peer, me).wait_send())
    for h in range(passes):
        others(lambda peer: second(h, peer, peer).wait_recv())
        for j in range(members):
            k = j % each
            c = passes - 1 - h if j < each else passes + h
            at = slice(k * share, (k + 1) * share), slice(c * 128, (c + 1) * 128)
            frames[at] = back[h, j, 0]
            cumulative[at] = back[h, j, 1]
    for h in range(passes):
        others(lambda peer: second(h, peer, me).wait_send())


def shards(pulses, offsets, geometry, counts):
    rows, cols, width = ROWS, COLS, BINS
    slots = pulses.shape[1]
    members = lax.axis_size("sub")
    constants = [jnp.asarray(t) for t in tables(width, rows, cols)]
    track = jnp.transpose(geometry, (1, 0, 2))
    smem = pl.BlockSpec(memory_space=pltpu.SMEM)
    vmem = pl.BlockSpec(memory_space=pltpu.VMEM)
    passes = cols // 256
    share = 4 * rows // members
    whole = jax.ShapeDtypeStruct((2 * rows, cols), jnp.float32)
    dma = pltpu.SemaphoreType.DMA((passes, members))
    win = pl.pallas_call(
        fetch_kernel,
        out_shape=jax.ShapeDtypeStruct((2 * slots, width), jnp.float32),
        in_specs=[smem, vmem],
        out_specs=vmem,
        compiler_params=pltpu.CompilerParams(vmem_limit_bytes=16 * 2**20),
    )(offsets, pulses)
    last = pulses.shape[3] // width - 2
    frames, cumulative = pl.pallas_call(
        functools.partial(kernel, members, last),
        out_shape=(whole, whole),
        in_specs=[smem] * 2 + [vmem] * 7,
        out_specs=(vmem, vmem),
        scratch_shapes=[
            pltpu.VMEM((2 * (rows // 8), slots, width), jnp.float32),
            pltpu.VMEM((slots // GROUP, 2 * rows, GROUP * width), jnp.bfloat16),
            pltpu.VMEM((4, slots, 8 + width // 16, 128), jnp.float32),
            pltpu.VMEM((2 * rows, 256), jnp.float32),
            pltpu.VMEM((2 * rows, width), jnp.float32),
            pltpu.VMEM((passes, members, share, 128), jnp.float32),
            pltpu.VMEM((passes, members, share, 128), jnp.float32),
            pltpu.VMEM((passes, members, 2, share, 128), jnp.float32),
            pltpu.VMEM((passes, members, 2, share, 128), jnp.float32),
            dma,
            dma,
            dma,
            dma,
        ],
        compiler_params=pltpu.CompilerParams(
            collective_id=0, has_side_effects=True, vmem_limit_bytes=16 * 2**20
        ),
    )(track, counts, win, offsets, track, *constants)
    return frames.reshape(1, 2, rows, cols), cumulative.reshape(1, 2, rows, cols)


def solution(mesh):
    return jax.shard_map(
        shards,
        mesh=mesh,
        in_specs=(
            P(("win", "sub"), None, None, None),
            P(("win", "sub"), None),
            P(("win", "sub"), None, None),
            P(("win", "sub")),
        ),
        out_specs=(P(("win", "sub"), None, None, None), P(("win", "sub"), None, None, None)),
        check_vma=False,
    )
```
